128 devices in a mesh: row: 16 (over y, x), col: 8 (over z, core).
Axes of the slice: x: 4, y: 4, z: 4, core: 2. Of those that a mesh axis runs over, the one named last changes fastest.
Arguments:
- cotangent: bfloat16 [49152, 256], P(('row', 'col')), may hold values from -6 to 6
- seed_label: int32 [49152], P(('row', 'col')), may hold values from 0 to 511
- tile_values: bfloat16 [16, 8, 16, 24, 128, 128], P('row', 'col'), may hold values from 0 to 0.008239746
- tile_rows: int32 [16, 8, 16, 24], P('row', 'col'), may hold values from 0 to 23
- tile_cols: int32 [16, 8, 16, 24], P('row', 'col'), may hold values from 0 to 2
- tile_scale: int32 [16, 8, 16, 24], P('row', 'col'), may hold values from 0 to 4
Outputs:
- first_grad: bfloat16 [49152, 256], P(('row', 'col'))
- label_grad: bfloat16 [49152, 256], P(('row', 'col'))
The draws below stay inside these ranges and needn't reach their ends.
All inputs are finite; a program needn't handle non-finite values.
Results may differ from the reference program's by a relative error of at most 0.019.
Values may be sent and summed in bfloat16 or wider, within the bound.
A program may use at most 64 MiB of HBM per device.

```python
import jax
import jax.numpy as jnp
from jax import lax

CLS = 256
TILE = 128
SEG = 384
TPR = 24
BPS = 3
NODES = 49152
N_ROW = 16
N_COL = 8


def touch_ends(array, key, smallest, top_value):
    longest = array.shape.index(max(array.shape))
    spots = []
    for shift in (0, 1):
        where = [jax.random.randint(jax.random.fold_in(key, axis), (), 0, length) for axis, length in enumerate(array.shape)]
        where[longest] = (where[longest] + shift) % array.shape[longest]
        spots.append(tuple(where))
    return array.at[spots[0]].set(smallest).at[spots[1]].set(top_value)


def level_of(rng, shape, pieces, low, top_value):
    gain, own = 1.0, jax.random.fold_in(rng, 6)
    for dim, shards_of in pieces:
        heights = jnp.exp(jax.random.uniform(jax.random.fold_in(own, dim), (shards_of,), jnp.float32, low / len(pieces), top_value / len(pieces)))
        gain = gain * jnp.repeat(heights, shape[dim] // shards_of).reshape([-1 if axis == dim else 1 for axis in range(len(shape))])
    return gain


def noise(stream_key, extent, deviation, most, shards=(), kind=jnp.bfloat16):
    drawn = jax.random.normal(stream_key, extent, jnp.float32) * deviation
    if len(shards) > 0:
        drawn = level_of(stream_key, extent, shards, -0.22, 0.18) * drawn
    return jnp.clip(drawn, min=-most, max=most).astype(kind)


def setup_inputs(seed: int = 0) -> dict:
    streams_of = jax.random.split(jax.random.key(seed), 7)
    cotangent = noise(streams_of[0], (NODES, CLS), 1.0, 6.0, ((0, 128),))
    seed_label = touch_ends(jax.random.randint(streams_of[1], (NODES,), 0, 2 * CLS), jax.random.fold_in(streams_of[1], 1), 0, (2 * CLS) - 1).astype(jnp.int32)
    tile_values = jnp.clip(0.008239746 * jax.random.uniform(streams_of[2], (N_ROW, N_COL, N_ROW, TPR, TILE, TILE), jnp.float32) ** level_of(streams_of[2], (N_ROW, N_COL, N_ROW, TPR, TILE, TILE), ((0, 16), (1, 8)), -0.2, 0.2), 0.0, 0.008239746).astype(jnp.bfloat16)
    tile_rows = touch_ends(jax.random.randint(streams_of[3], (N_ROW, N_COL, N_ROW, TPR), 0, N_COL * BPS), jax.random.fold_in(streams_of[3], 1), 0, (N_COL * BPS) - 1).astype(jnp.int32)
    tile_cols = touch_ends(jax.random.randint(streams_of[4], (N_ROW, N_COL, N_ROW, TPR), 0, BPS), jax.random.fold_in(streams_of[4], 1), 0, BPS - 1).astype(jnp.int32)
    tile_scale = touch_ends(jax.random.randint(streams_of[5], (N_ROW, N_COL, N_ROW, TPR), 0, 5), jax.random.fold_in(streams_of[5], 1), 0, 4).astype(jnp.int32)
    return dict(cotangent=cotangent, seed_label=seed_label, tile_values=tile_values, tile_rows=tile_rows, tile_cols=tile_cols, tile_scale=tile_scale)


ALPHA = 0.9


def group_term(sources, tile_block, row_ids, col_ids, scale_ids):
    blocks = SEG // TILE
    picked = jnp.take(sources, row_ids, axis=0)
    products = jnp.einsum("tij,tic->tjc", tile_block.astype(jnp.float32), picked.astype(jnp.float32), precision=lax.Precision.HIGHEST)
    weights = scale_ids.astype(jnp.float32)[:, None] * (col_ids[:, None] == jnp.arange(blocks, dtype=jnp.int32)[None, :]).astype(jnp.float32)
    summed = jnp.einsum("tb,tjc->bjc", weights, products, precision=lax.Precision.HIGHEST)
    return summed.reshape(SEG, CLS)


def propagate(labels, tile_values, tile_rows, tile_cols, tile_scale):
    accum = jnp.zeros((N_ROW, N_COL, SEG, CLS), jnp.float32)

    def visit(device, accum):
        device = jnp.asarray(device).astype(jnp.int32)
        row_pos = device // N_COL
        col_pos = device % N_COL
        begin = (row_pos * (N_COL * SEG)).astype(jnp.int32)
        sources = lax.dynamic_slice_in_dim(labels, begin, N_COL * SEG, 0).reshape(N_COL * SEG // TILE, TILE, CLS)
        tile_item = (tile_values[row_pos, col_pos], tile_rows[row_pos, col_pos], tile_cols[row_pos, col_pos], tile_scale[row_pos, col_pos])
        group_sums = lax.map(lambda member: group_term(sources, member[0], member[1], member[2], member[3]), tile_item)
        rounded = lax.optimization_barrier(group_sums.astype(jnp.bfloat16)).astype(jnp.float32)
        zero = jnp.zeros((), jnp.int32)
        current = lax.dynamic_slice(accum, (zero, col_pos, zero, zero), (N_ROW, 1, SEG, CLS))
        return lax.dynamic_update_slice(accum, current + rounded[:, None], (zero, col_pos, zero, zero))

    accum = lax.fori_loop(0, N_ROW * N_COL, visit, accum)
    return accum.reshape(NODES, CLS)


def reference(cotangent, seed_label, tile_values, tile_rows, tile_cols, tile_scale):
    keep_mask = (seed_label[:, None] != jnp.arange(CLS, dtype=jnp.int32)[None, :]).astype(jnp.float32)
    first_in = (cotangent.astype(jnp.float32) * keep_mask).astype(jnp.bfloat16)
    first_grad = (ALPHA * propagate(first_in, tile_values, tile_rows, tile_cols, tile_scale)).astype(jnp.bfloat16)
    second_in = (first_grad.astype(jnp.float32) * keep_mask).astype(jnp.bfloat16)
    second = propagate(second_in, tile_values, tile_rows, tile_cols, tile_scale)
    label_grad = ALPHA * second + (1.0 - ALPHA) * keep_mask * (cotangent.astype(jnp.float32) + first_grad.astype(jnp.float32))
    return first_grad, label_grad.astype(jnp.bfloat16)
```

```python
import functools

import jax
import jax.numpy as jnp
from jax import lax
from jax.experimental import pallas as pl
from jax.experimental.pallas import tpu as pltpu
from jax.sharding import PartitionSpec as P

ALPHA = 0.9
MESH = pl.DeviceIdType.MESH
F32 = jnp.float32
BF16 = jnp.bfloat16
RING = 4
TN = (((0,), (0,)), ((), ()))
N_REDUCE = 20
N_GATHER = 13


def sorted_slots(rows, cols, scale):
    groups, slots = rows.shape
    index = jnp.arange(slots, dtype=jnp.int32)[None, :]
    keys = cols * slots + index
    rank = jnp.sum((keys[:, None, :] < keys[:, :, None]).astype(jnp.int32), axis=2)
    placed = rank[:, :, None] == jnp.arange(slots, dtype=jnp.int32)[None, None, :]
    tile = jnp.arange(groups, dtype=jnp.int32)[:, None] * slots + index
    parts = [jnp.sum(jnp.where(placed, v[:, :, None], 0), axis=1) for v in (tile, rows, scale)]
    first = jnp.sum((cols < 1).astype(jnp.int32), axis=1, keepdims=True)
    second = jnp.sum((cols < 2).astype(jnp.int32), axis=1, keepdims=True)
    return jnp.concatenate(parts + [first, second], axis=1)


def kernel(
    cot_ref, seed_ref, order, tiles_hbm,
    first_ref, label_ref,
    tiles, gathered0, gathered1, prefix0, prefix1, current, own, sent, got, keep,
    tile_sem, send_sem, recv_sem,
):
    tile = tiles.shape[1]
    groups = order.shape[0]
    slots = tiles.shape[0] // groups
    gathered = (gathered0, gathered1)
    prefix = (prefix0, prefix1)
    sub = gathered0.shape[1]
    segment, classes = cot_ref.shape
    half = segment // 2
    per = segment // sub
    row, col = lax.axis_index("row"), lax.axis_index("col")
    y, x = row // RING, row % RING
    z, core = col // 2, col % 2
    a = x + core * (y - x)
    b = y + core * (x - y)
    step_a = 1 + 3 * core
    step_b = 4 - 3 * core

    def at(da, db):
        return ((a + da) % RING) * step_a + ((b + db) % RING) * step_b

    def device(da, db):
        return {"row": at(da, db), "col": col}

    a_right, a_left = device(1, 0), device(3, 0)
    b_right, b_left = device(0, 1), device(0, 3)
    z_right = {"row": row, "col": ((z + 1) % RING) * 2 + core}
    z_left = {"row": row, "col": ((z + 3) % RING) * 2 + core}
    twin = {"row": row, "col": z * 2 + (1 - core)}

    loads = [
        pltpu.make_async_copy(
            tiles_hbm.at[pl.ds(q * tiles.shape[0] // 4, tiles.shape[0] // 4)],
            tiles.at[pl.ds(q * tiles.shape[0] // 4, tiles.shape[0] // 4)],
            tile_sem.at[q],
        )
        for q in range(4)
    ]
    for load in loads:
        load.start()

    barrier = pltpu.get_barrier_semaphore()
    for other in (a_right, a_left, b_right, b_left, z_right, z_left, twin):
        pl.semaphore_signal(barrier, inc=1, device_id=other, device_id_type=MESH)

    for block in range(segment // tile):
        seeds = jnp.broadcast_to(seed_ref[block : block + 1, :], (tile, tile)).T
        lanes = lax.broadcasted_iota(jnp.int32, (tile, tile), 1)
        rows = slice(block * tile, (block + 1) * tile)
        for c in range(classes // tile):
            lane = slice(c * tile, (c + 1) * tile)
            kept = jnp.where(seeds == lanes + c * tile, 0.0, 1.0)
            keep[rows, lane] = kept
            masked = (cot_ref[rows, lane].astype(F32) * kept).astype(BF16)
            for part in range(tile // sub):
                gathered0[col * per + block * (tile // sub) + part, :, lane] = masked[part * sub : (part + 1) * sub]

    pl.semaphore_wait(barrier, 7)

    def gather_copy(p, j):
        seg_left = ((z + 3) % RING) * 2 + core
        seg_right = ((z + 1) % RING) * 2 + core
        seg_far = ((z + 2) % RING) * 2 + core
        seg, top, size, target = (
            (col, 0, half, z_right),
            (col, half, half, z_right),
            (col, half, half, z_left),
            (col, 0, half, z_left),
            (seg_left, 0, half, z_right),
            (seg_right, half, half, z_left),
            (col, 0, segment, twin),
            (seg_left, 0, half, twin),
            (seg_left, half, half, twin),
            (seg_right, half, half, twin),
            (seg_right, 0, half, twin),
            (seg_far, 0, half, twin),
            (seg_far, half, half, twin),
        )[j]
        window = gathered[p].at[pl.ds(seg * per + top // sub, size // sub)]
        sem = N_REDUCE + j
        return pltpu.make_async_remote_copy(
            src_ref=window, dst_ref=window, send_sem=send_sem.at[p, sem], recv_sem=recv_sem.at[p, sem],
            device_id=target, device_id_type=MESH,
        )

    def arrival(p, j):
        seg_left = ((z + 3) % RING) * 2 + core
        seg_right = ((z + 1) % RING) * 2 + core
        seg_far = ((z + 2) % RING) * 2 + core
        flip = 1 - 2 * core
        seg, top, size = (
            (seg_left, 0, half),
            (seg_left, half, half),
            (seg_right, half, half),
            (seg_right, 0, half),
            (seg_far, 0, half),
            (seg_far, half, half),
            (col + flip, 0, segment),
            (seg_left + flip, 0, half),
            (seg_left + flip, half, half),
            (seg_right + flip, half, half),
            (seg_right + flip, 0, half),
            (seg_far + flip, 0, half),
            (seg_far + flip, half, half),
        )[j]
        window = gathered[p].at[pl.ds(seg * per + top // sub, size // sub)]
        sem = N_REDUCE + j
        return pltpu.make_async_remote_copy(
            src_ref=window, dst_ref=window, send_sem=send_sem.at[p, sem], recv_sem=recv_sem.at[p, sem],
            device_id=twin, device_id_type=MESH,
        )

    def reduce_copy(p, i, kind, right, left):
        piece = max(kind - 1, 0)
        rows = (pl.ds(0, half), pl.ds(half, half), pl.ds(0, segment), pl.ds(0, segment))[kind]
        sem = 4 * i + kind
        return pltpu.make_async_remote_copy(
            src_ref=sent.at[p, 3 * i + piece, rows], dst_ref=got.at[p, 3 * i + piece, rows],
            send_sem=send_sem.at[p, sem], recv_sem=recv_sem.at[p, sem],
            device_id=(right, left, right, left)[kind], device_id_type=MESH,
        )

    def start_gather(p):
        for j in (0, 2, 6, 1, 3):
            gather_copy(p, j).start()

    def finish_gather(p):
        arrival(p, 0).wait_recv()
        gather_copy(p, 4).start()
        gather_copy(p, 7).start()
        arrival(p, 2).wait_recv()
        gather_copy(p, 5).start()
        gather_copy(p, 9).start()
        arrival(p, 1).wait_recv()
        gather_copy(p, 8).start()
        arrival(p, 3).wait_recv()
        gather_copy(p, 10).start()
        arrival(p, 4).wait_recv()
        gather_copy(p, 11).start()
        arrival(p, 5).wait_recv()
        gather_copy(p, 12).start()
        for j in range(6, N_GATHER):
            arrival(p, j).wait_recv()

    start_gather(0)

    def product(p, u, target):
        total = jnp.zeros((tile, classes), F32)
        prefix[u][0] = total
        for q in range(slots):
            source = order[target, slots + q] * (tile // sub)
            labels = jnp.concatenate([gathered[p][source + part] for part in range(tile // sub)], axis=0)
            term = lax.dot_general(tiles[order[target, q]], labels, TN, preferred_element_type=F32)
            total = total + term * order[target, 2 * slots + q].astype(F32)
            prefix[u][q + 1] = total
        one = prefix[u][order[target, 3 * slots]]
        two = prefix[u][order[target, 3 * slots + 1]]
        current[u, 0:tile] = one
        current[u, tile : 2 * tile] = two - one
        current[u, 2 * tile : 3 * tile] = total - two

    upper, lower, whole = pl.ds(0, half), pl.ds(half, half), pl.ds(0, segment)

    def summed(p, i):
        reduce_copy(p, i, 2, a_right, a_left).wait_recv()
        reduce_copy(p, i, 3, a_right, a_left).wait_recv()
        return own[i] + got[p, 3 * i + 1].astype(F32) + got[p, 3 * i + 2].astype(F32)

    for p in range(2):
        finish_gather(p)
        if p == 0:
            for load in loads:
                load.wait()

        def one_step(s, carry):
            far = s < 2
            side = jnp.logical_and(s >= 2, s < 6)
            i0 = jnp.where(far, 2 * s, jnp.where(side, s - 2, 2 * s - 12))
            i1 = jnp.where(side, i0, i0 + 1)
            da0 = jnp.where(far, 2, jnp.where(side, 1, 0))
            da1 = jnp.where(far, 2, jnp.where(side, 3, 0))
            product(p, 0, at(da0, 2 + i0 * (i0 + 1) // 2))
            product(p, 1, at(da1, 2 + i1 * (i1 + 1) // 2))

            @pl.when(far)
            def _():
                for u in range(2):
                    i = 2 * s + u
                    sent[p, 3 * i] = current[u].astype(BF16)
                    reduce_copy(p, i, 0, a_right, a_left).start()
                    reduce_copy(p, i, 1, a_right, a_left).start()

            @pl.when(side)
            def _():
                i = s - 2
                sent[p, 3 * i + 1, half:segment] = current[0, half:segment].astype(BF16)
                sent[p, 3 * i + 2, 0:half] = current[1, 0:half].astype(BF16)
                reduce_copy(p, i, 0, a_right, a_left).wait_recv()
                sent[p, 3 * i + 1, 0:half] = (current[0, 0:half] + got[p, 3 * i, 0:half].astype(F32)).astype(BF16)
                reduce_copy(p, i, 2, a_right, a_left).start()
                reduce_copy(p, i, 1, a_right, a_left).wait_recv()
                sent[p, 3 * i + 2, half:segment] = (
                    current[1, half:segment] + got[p, 3 * i, half:segment].astype(F32)
                ).astype(BF16)
                reduce_copy(p, i, 3, a_right, a_left).start()

            @pl.when(s >= 6)
            def _():
                own[2 * s - 12] = current[0]
                own[2 * s - 11] = current[1]

            @pl.when(s == 6)
            def _():
                sent[p, 12] = summed(p, 0).astype(BF16)
                reduce_copy(p, 4, 0, b_right, b_left).start()
                reduce_copy(p, 4, 1, b_right, b_left).start()

            return carry

        lax.fori_loop(0, 8, one_step, 0)

        total = summed(p, 1)
        reduce_copy(p, 4, 1, b_right, b_left).wait_recv()
        sent[p, 14, 0:half] = total[0:half].astype(BF16)
        sent[p, 14, half:segment] = (total[half:segment] + got[p, 12, half:segment].astype(F32)).astype(BF16)
        reduce_copy(p, 4, 3, b_right, b_left).start()
        total = summed(p, 2)
        reduce_copy(p, 4, 0, b_right, b_left).wait_recv()
        sent[p, 13, half:segment] = total[half:segment].astype(BF16)
        sent[p, 13, 0:half] = (total[0:half] + got[p, 12, 0:half].astype(F32)).astype(BF16)
        reduce_copy(p, 4, 2, b_right, b_left).start()
        own[3] = summed(p, 3)
        reduce_copy(p, 4, 2, b_right, b_left).wait_recv()
        reduce_copy(p, 4, 3, b_right, b_left).wait_recv()
        own[3] = ALPHA * (own[3] + got[p, 13].astype(F32) + got[p, 14].astype(F32))

        if p == 0:
            first = own[3].astype(BF16)
            first_ref[...] = first
            masked = (first.astype(F32) * keep[...]).astype(BF16)
            for part in range(per):
                gathered1[col * per + part] = masked[part * sub : (part + 1) * sub]
            start_gather(1)
        else:
            label_ref[...] = (
                own[3] + (1.0 - ALPHA) * keep[...] * (cot_ref[...].astype(F32) + first_ref[...].astype(F32))
            ).astype(BF16)

    for p in range(2):
        for j in range(N_GATHER):
            gather_copy(p, j).wait_send()
        for i in range(5):
            right, left = (a_right, a_left) if i < 4 else (b_right, b_left)
            for kind in range(4):
                reduce_copy(p, i, kind, right, left).wait_send()


def local(cotangent, seed_label, tile_values, tile_rows, tile_cols, tile_scale):
    segment, classes = cotangent.shape
    _, _, groups, slots, tile, _ = tile_values.shape
    vmem, smem = pl.BlockSpec(memory_space=pltpu.VMEM), pl.BlockSpec(memory_space=pltpu.SMEM)
    out = jax.ShapeDtypeStruct((segment, classes), BF16)
    return pl.pallas_call(
        kernel,
        out_shape=(out, out),
        in_specs=[vmem, vmem, smem, pl.BlockSpec(memory_space=pl.ANY)],
        out_specs=(vmem, vmem),
        scratch_shapes=[
            pltpu.VMEM((groups * slots, tile, tile), BF16),
            pltpu.VMEM((2 * RING * segment // 64, 64, classes), BF16),
            pltpu.VMEM((2 * RING * segment // 64, 64, classes), BF16),
            pltpu.VMEM((slots + 1, tile, classes), F32),
            pltpu.VMEM((slots + 1, tile, classes), F32),
            pltpu.VMEM((2, segment, classes), F32),
            pltpu.VMEM((4, segment, classes), F32),
            pltpu.VMEM((2, 15, segment, classes), BF16),
            pltpu.VMEM((2, 15, segment, classes), BF16),
            pltpu.VMEM((segment, classes), F32),
            pltpu.SemaphoreType.DMA((4,)),
            pltpu.SemaphoreType.DMA((2, N_REDUCE + N_GATHER)),
            pltpu.SemaphoreType.DMA((2, N_REDUCE + N_GATHER)),
        ],
        compiler_params=pltpu.CompilerParams(
            collective_id=0, has_side_effects=True, vmem_limit_bytes=56 * 1024 * 1024
        ),
        name="propagate_twice",
    )(
        cotangent,
        seed_label.reshape(segment // tile, tile),
        sorted_slots(tile_rows[0, 0], tile_cols[0, 0], tile_scale[0, 0]),
        tile_values.reshape(groups * slots, tile, tile),
    )


def solution(mesh):
    return jax.shard_map(
        local,
        mesh=mesh,
        in_specs=(
            P(("row", "col"), None),
            P(("row", "col")),
            P("row", "col", None, None, None, None),
            P("row", "col", None, None),
            P("row", "col", None, None),
            P("row", "col", None, None),
        ),
        out_specs=(P(("row", "col"), None), P(("row", "col"), None)),
        check_vma=False,
    )
```

```python
import functools

import jax
import jax.numpy as jnp
from jax import lax
from jax.experimental import pallas as pl
from jax.experimental.pallas import tpu as pltpu
from jax.sharding import PartitionSpec as P

ALPHA = 0.9
MESH = pl.DeviceIdType.MESH
F32 = jnp.float32
BF16 = jnp.bfloat16
RING = 4
TN = (((0,), (0,)), ((), ()))
N_REDUCE = 20
N_GATHER = 13


def sort_network(count):
    size = 1
    while size < count:
        size *= 2
    pairs = []
    p = 1
    while p < size:
        k = p
        while k >= 1:
            for j in range(k % p, size - k, 2 * k):
                for i in range(min(k, size - j - k)):
                    if (i + j) // (p * 2) == (i + j + k) // (p * 2) and i + j + k < count:
                        pairs.append((i + j, i + j + k))
            k //= 2
        p *= 2
    return pairs


def kernel(
    cot_ref, seed_ref, rows_ref, cols_ref, scale_ref, tiles_hbm,
    first_ref, label_ref,
    tiles, gathered0, gathered1, prefix0, prefix1, current, own, sent, got, keep, order,
    tile_sem, send_sem, recv_sem,
):
    tile = tiles.shape[1]
    groups = rows_ref.shape[0]
    slots = tiles.shape[0] // groups
    gathered = (gathered0, gathered1)
    prefix = (prefix0, prefix1)
    sub = gathered0.shape[1]
    segment, classes = cot_ref.shape
    half = segment // 2
    per = segment // sub
    row, col = lax.axis_index("row"), lax.axis_index("col")
    y, x = row // RING, row % RING
    z, core = col // 2, col % 2
    a = x + core * (y - x)
    b = y + core * (x - y)
    step_a = 1 + 3 * core
    step_b = 4 - 3 * core

    def at(da, db):
        return ((a + da) % RING) * step_a + ((b + db) % RING) * step_b

    def device(da, db):
        return {"row": at(da, db), "col": col}

    a_right, a_left = device(1, 0), device(3, 0)
    b_right, b_left = device(0, 1), device(0, 3)
    z_right = {"row": row, "col": ((z + 1) % RING) * 2 + core}
    z_left = {"row": row, "col": ((z + 3) % RING) * 2 + core}
    twin = {"row": row, "col": z * 2 + (1 - core)}

    loads = [
        pltpu.make_async_copy(
            tiles_hbm.at[pl.ds(q * tiles.shape[0] // 4, tiles.shape[0] // 4)],
            tiles.at[pl.ds(q * tiles.shape[0] // 4, tiles.shape[0] // 4)],
            tile_sem.at[q],
        )
        for q in range(4)
    ]
    for load in loads:
        load.start()

    barrier = pltpu.get_barrier_semaphore()
    for other in (a_right, a_left, b_right, b_left, z_right, z_left, twin):
        pl.semaphore_signal(barrier, inc=1, device_id=other, device_id_type=MESH)

    for block in range(segment // tile):
        seeds = jnp.broadcast_to(seed_ref[block : block + 1, :], (tile, tile)).T
        lanes = lax.broadcasted_iota(jnp.int32, (tile, tile), 1)
        rows = slice(block * tile, (block + 1) * tile)
        for c in range(classes // tile):
            lane = slice(c * tile, (c + 1) * tile)
            kept = jnp.where(seeds == lanes + c * tile, 0.0, 1.0)
            keep[rows, lane] = kept
            masked = (cot_ref[rows, lane].astype(F32) * kept).astype(BF16)
            for part in range(tile // sub):
                gathered0[col * per + block * (tile // sub) + part, :, lane] = masked[part * sub : (part + 1) * sub]

    pl.semaphore_wait(barrier, 7)

    def gather_copy(p, j):
        seg_left = ((z + 3) % RING) * 2 + core
        seg_right = ((z + 1) % RING) * 2 + core
        seg_far = ((z + 2) % RING) * 2 + core
        seg, top, size, target = (
            (col, 0, half, z_right),
            (col, half, half, z_right),
            (col, half, half, z_left),
            (col, 0, half, z_left),
            (seg_left, 0, half, z_right),
            (seg_right, half, half, z_left),
            (col, 0, segment, twin),
            (seg_left, 0, half, twin),
            (seg_left, half, half, twin),
            (seg_right, half, half, twin),
            (seg_right, 0, half, twin),
            (seg_far, 0, half, twin),
            (seg_far, half, half, twin),
        )[j]
        window = gathered[p].at[pl.ds(seg * per + top // sub, size // sub)]
        sem = N_REDUCE + j
        return pltpu.make_async_remote_copy(
            src_ref=window, dst_ref=window, send_sem=send_sem.at[p, sem], recv_sem=recv_sem.at[p, sem],
            device_id=target, device_id_type=MESH,
        )

    def arrival(p, j):
        seg_left = ((z + 3) % RING) * 2 + core
        seg_right = ((z + 1) % RING) * 2 + core
        seg_far = ((z + 2) % RING) * 2 + core
        flip = 1 - 2 * core
        seg, top, size = (
            (seg_left, 0, half),
            (seg_left, half, half),
            (seg_right, half, half),
            (seg_right, 0, half),
            (seg_far, 0, half),
            (seg_far, half, half),
            (col + flip, 0, segment),
            (seg_left + flip, 0, half),
            (seg_left + flip, half, half),
            (seg_right + flip, half, half),
            (seg_right + flip, 0, half),
            (seg_far + flip, 0, half),
            (seg_far + flip, half, half),
        )[j]
        window = gathered[p].at[pl.ds(seg * per + top // sub, size // sub)]
        sem = N_REDUCE + j
        return pltpu.make_async_remote_copy(
            src_ref=window, dst_ref=window, send_sem=send_sem.at[p, sem], recv_sem=recv_sem.at[p, sem],
            device_id=twin, device_id_type=MESH,
        )

    def reduce_copy(p, i, kind, right, left):
        piece = max(kind - 1, 0)
        rows = (pl.ds(0, half), pl.ds(half, half), pl.ds(0, segment), pl.ds(0, segment))[kind]
        sem = 4 * i + kind
        return pltpu.make_async_remote_copy(
            src_ref=sent.at[p, 3 * i + piece, rows], dst_ref=got.at[p, 3 * i + piece, rows],
            send_sem=send_sem.at[p, sem], recv_sem=recv_sem.at[p, sem],
            device_id=(right, left, right, left)[kind], device_id_type=MESH,
        )

    def start_gather(p):
        for j in (0, 2, 6, 1, 3):
            gather_copy(p, j).start()

    def finish_gather(p):
        arrival(p, 0).wait_recv()
        gather_copy(p, 4).start()
        gather_copy(p, 7).start()
        arrival(p, 2).wait_recv()
        gather_copy(p, 5).start()
        gather_copy(p, 9).start()
        arrival(p, 1).wait_recv()
        gather_copy(p, 8).start()
        arrival(p, 3).wait_recv()
        gather_copy(p, 10).start()
        arrival(p, 4).wait_recv()
        gather_copy(p, 11).start()
        arrival(p, 5).wait_recv()
        gather_copy(p, 12).start()
        for j in range(6, N_GATHER):
            arrival(p, j).wait_recv()

    start_gather(0)

    def sort_group(g, carry):
        keys, first, second = [], 0, 0
        for k in range(slots):
            c = cols_ref[g, k]
            keys.append(c * 8192 + (k * 256 + rows_ref[g, k] * 8 + scale_ref[g, k]))
            first = first + ((2 - c) >> 1)
            second = second + (1 - (c >> 1))
        for i, j in sort_network(slots):
            keys[i], keys[j] = jnp.minimum(keys[i], keys[j]), jnp.maximum(keys[i], keys[j])
        for k in range(slots):
            order[g, k] = ((keys[k] >> 8) & 31) + g * slots
            order[g, slots + k] = (keys[k] >> 3) & 31
            order[g, 2 * slots + k] = keys[k] & 7
        order[g, 3 * slots] = first
        order[g, 3 * slots + 1] = second
        return carry

    lax.fori_loop(0, groups, sort_group, 0)

    def product(p, u, target):
        total = jnp.zeros((tile, classes), F32)
        prefix[u][0] = total
        for q in range(slots):
            source = order[target, slots + q] * (tile // sub)
            labels = jnp.concatenate([gathered[p][source + part] for part in range(tile // sub)], axis=0)
            term = lax.dot_general(tiles[order[target, q]], labels, TN, preferred_element_type=F32)
            total = total + term * order[target, 2 * slots + q].astype(F32)
            prefix[u][q + 1] = total
        one = prefix[u][order[target, 3 * slots]]
        two = prefix[u][order[target, 3 * slots + 1]]
        current[u, 0:tile] = one
        current[u, tile : 2 * tile] = two - one
        current[u, 2 * tile : 3 * tile] = total - two

    upper, lower, whole = pl.ds(0, half), pl.ds(half, half), pl.ds(0, segment)

    def summed(p, i):
        reduce_copy(p, i, 2, a_right, a_left).wait_recv()
        reduce_copy(p, i, 3, a_right, a_left).wait_recv()
        return own[i] + got[p, 3 * i + 1].astype(F32) + got[p, 3 * i + 2].astype(F32)

    for p in range(2):
        finish_gather(p)
        if p == 0:
            for load in loads:
                load.wait()

        def one_step(s, carry):
            far = s < 2
            side = jnp.logical_and(s >= 2, s < 6)
            i0 = jnp.where(far, 2 * s, jnp.where(side, s - 2, 2 * s - 12))
            i1 = jnp.where(side, i0, i0 + 1)
            da0 = jnp.where(far, 2, jnp.where(side, 1, 0))
            da1 = jnp.where(far, 2, jnp.where(side, 3, 0))
            product(p, 0, at(da0, 2 + i0 * (i0 + 1) // 2))
            product(p, 1, at(da1, 2 + i1 * (i1 + 1) // 2))

            @pl.when(far)
            def _():
                for u in range(2):
                    i = 2 * s + u
                    sent[p, 3 * i] = current[u].astype(BF16)
                    reduce_copy(p, i, 0, a_right, a_left).start()
                    reduce_copy(p, i, 1, a_right, a_left).start()

            @pl.when(side)
            def _():
                i = s - 2
                sent[p, 3 * i + 1, half:segment] = current[0, half:segment].astype(BF16)
                sent[p, 3 * i + 2, 0:half] = current[1, 0:half].astype(BF16)
                reduce_copy(p, i, 0, a_right, a_left).wait_recv()
                sent[p, 3 * i + 1, 0:half] = (current[0, 0:half] + got[p, 3 * i, 0:half].astype(F32)).astype(BF16)
                reduce_copy(p, i, 2, a_right, a_left).start()
                reduce_copy(p, i, 1, a_right, a_left).wait_recv()
                sent[p, 3 * i + 2, half:segment] = (
                    current[1, half:segment] + got[p, 3 * i, half:segment].astype(F32)
                ).astype(BF16)
                reduce_copy(p, i, 3, a_right, a_left).start()

            @pl.when(s >= 6)
            def _():
                own[2 * s - 12] = current[0]
                own[2 * s - 11] = current[1]

            @pl.when(s == 6)
            def _():
                sent[p, 12] = summed(p, 0).astype(BF16)
                reduce_copy(p, 4, 0, b_right, b_left).start()
                reduce_copy(p, 4, 1, b_right, b_left).start()

            return carry

        lax.fori_loop(0, 8, one_step, 0)

        total = summed(p, 1)
        reduce_copy(p, 4, 1, b_right, b_left).wait_recv()
        sent[p, 14, 0:half] = total[0:half].astype(BF16)
        sent[p, 14, half:segment] = (total[half:segment] + got[p, 12, half:segment].astype(F32)).astype(BF16)
        reduce_copy(p, 4, 3, b_right, b_left).start()
        total = summed(p, 2)
        reduce_copy(p, 4, 0, b_right, b_left).wait_recv()
        sent[p, 13, half:segment] = total[half:segment].astype(BF16)
        sent[p, 13, 0:half] = (total[0:half] + got[p, 12, 0:half].astype(F32)).astype(BF16)
        reduce_copy(p, 4, 2, b_right, b_left).start()
        own[3] = summed(p, 3)
        reduce_copy(p, 4, 2, b_right, b_left).wait_recv()
        reduce_copy(p, 4, 3, b_right, b_left).wait_recv()
        own[3] = ALPHA * (own[3] + got[p, 13].astype(F32) + got[p, 14].astype(F32))

        if p == 0:
            first = own[3].astype(BF16)
            first_ref[...] = first
            masked = (first.astype(F32) * keep[...]).astype(BF16)
            for part in range(per):
                gathered1[col * per + part] = masked[part * sub : (part + 1) * sub]
            start_gather(1)
        else:
            label_ref[...] = (
                own[3] + (1.0 - ALPHA) * keep[...] * (cot_ref[...].astype(F32) + first_ref[...].astype(F32))
            ).astype(BF16)

    for p in range(2):
        for j in range(N_GATHER):
            gather_copy(p, j).wait_send()
        for i in range(5):
            right, left = (a_right, a_left) if i < 4 else (b_right, b_left)
            for kind in range(4):
                reduce_copy(p, i, kind, right, left).wait_send()


def local(cotangent, seed_label, tile_values, tile_rows, tile_cols, tile_scale):
    segment, classes = cotangent.shape
    _, _, groups, slots, tile, _ = tile_values.shape
    vmem, smem = pl.BlockSpec(memory_space=pltpu.VMEM), pl.BlockSpec(memory_space=pltpu.SMEM)
    out = jax.ShapeDtypeStruct((segment, classes), BF16)
    return pl.pallas_call(
        kernel,
        out_shape=(out, out),
        in_specs=[vmem, vmem, smem, smem, smem, pl.BlockSpec(memory_space=pl.ANY)],
        out_specs=(vmem, vmem),
        scratch_shapes=[
            pltpu.VMEM((groups * slots, tile, tile), BF16),
            pltpu.VMEM((2 * RING * segment // 64, 64, classes), BF16),
            pltpu.VMEM((2 * RING * segment // 64, 64, classes), BF16),
            pltpu.VMEM((slots + 1, tile, classes), F32),
            pltpu.VMEM((slots + 1, tile, classes), F32),
            pltpu.VMEM((2, segment, classes), F32),
            pltpu.VMEM((4, segment, classes), F32),
            pltpu.VMEM((2, 15, segment, classes), BF16),
            pltpu.VMEM((2, 15, segment, classes), BF16),
            pltpu.VMEM((segment, classes), F32),
            pltpu.SMEM((groups, 3 * slots + 2), jnp.int32),
            pltpu.SemaphoreType.DMA((4,)),
            pltpu.SemaphoreType.DMA((2, N_REDUCE + N_GATHER)),
            pltpu.SemaphoreType.DMA((2, N_REDUCE + N_GATHER)),
        ],
        compiler_params=pltpu.CompilerParams(
            collective_id=0, has_side_effects=True, vmem_limit_bytes=56 * 1024 * 1024
        ),
        name="propagate_twice",
    )(
        cotangent,
        seed_label.reshape(segment // tile, tile),
        tile_rows[0, 0],
        tile_cols[0, 0],
        tile_scale[0, 0],
        tile_values.reshape(groups * slots, tile, tile),
    )


def solution(mesh):
    return jax.shard_map(
        local,
        mesh=mesh,
        in_specs=(
            P(("row", "col"), None),
            P(("row", "col")),
            P("row", "col", None, None, None, None),
            P("row", "col", None, None),
            P("row", "col", None, None),
            P("row", "col", None, None),
        ),
        out_specs=(P(("row", "col"), None), P(("row", "col"), None)),
        check_vma=False,
    )
```

```python
import functools

import jax
import jax.numpy as jnp
from jax import lax
from jax.experimental import pallas as pl
from jax.experimental.pallas import tpu as pltpu
from jax.sharding import PartitionSpec as P

ALPHA = 0.9
MESH = pl.DeviceIdType.MESH
F32 = jnp.float32
BF16 = jnp.bfloat16
RING = 4
TN = (((0,), (0,)), ((), ()))
N_REDUCE = 20
N_GATHER = 13


def sort_network(count):
    size = 1
    while size < count:
        size *= 2
    pairs = []
    p = 1
    while p < size:
        k = p
        while k >= 1:
            for j in range(k % p, size - k, 2 * k):
                for i in range(min(k, size - j - k)):
                    if (i + j) // (p * 2) == (i + j + k) // (p * 2) and i + j + k < count:
                        pairs.append((i + j, i + j + k))
            k //= 2
        p *= 2
    return pairs


def kernel(
    cot_ref, seed_ref, rows_ref, cols_ref, scale_ref, tiles_hbm,
    first_ref, label_ref,
    tiles, gathered0, gathered1, prefix0, prefix1, current, own, sent, got, keep, order,
    tile_sem, send_sem, recv_sem,
):
    tile = tiles.shape[1]
    groups = rows_ref.shape[0]
    slots = tiles.shape[0] // groups
    gathered = (gathered0, gathered1)
    prefix = (prefix0, prefix1)
    sub = gathered0.shape[1]
    segment, classes = cot_ref.shape
    half = segment // 2
    per = segment // sub
    row, col = lax.axis_index("row"), lax.axis_index("col")
    y, x = row // RING, row % RING
    z, core = col // 2, col % 2
    a = x + core * (y - x)
    b = y + core * (x - y)
    step_a = 1 + 3 * core
    step_b = 4 - 3 * core

    def at(da, db):
        return ((a + da) % RING) * step_a + ((b + db) % RING) * step_b

    def device(da, db):
        return {"row": at(da, db), "col": col}

    a_right, a_left = device(1, 0), device(3, 0)
    b_right, b_left = device(0, 1), device(0, 3)
    z_right = {"row": row, "col": ((z + 1) % RING) * 2 + core}
    z_left = {"row": row, "col": ((z + 3) % RING) * 2 + core}
    twin = {"row": row, "col": z * 2 + (1 - core)}

    loads = [
        pltpu.make_async_copy(
            tiles_hbm.at[pl.ds(q * tiles.shape[0] // 4, tiles.shape[0] // 4)],
            tiles.at[pl.ds(q * tiles.shape[0] // 4, tiles.shape[0] // 4)],
            tile_sem.at[q],
        )
        for q in range(4)
    ]
    for load in loads:
        load.start()

    barrier = pltpu.get_barrier_semaphore()
    for other in (a_right, a_left, b_right, b_left, z_right, z_left, twin):
        pl.semaphore_signal(barrier, inc=1, device_id=other, device_id_type=MESH)

    for block in range(segment // tile):
        seeds = jnp.broadcast_to(seed_ref[block : block + 1, :], (tile, tile)).T
        lanes = lax.broadcasted_iota(jnp.int32, (tile, tile), 1)
        rows = slice(block * tile, (block + 1) * tile)
        for c in range(classes // tile):
            lane = slice(c * tile, (c + 1) * tile)
            kept = jnp.where(seeds == lanes + c * tile, 0.0, 1.0)
            keep[rows, lane] = kept
            masked = (cot_ref[rows, lane].astype(F32) * kept).astype(BF16)
            for part in range(tile // sub):
                gathered0[col * per + block * (tile // sub) + part, :, lane] = masked[part * sub : (part + 1) * sub]

    pl.semaphore_wait(barrier, 7)

    def gather_copy(p, j):
        seg_left = ((z + 3) % RING) * 2 + core
        seg_right = ((z + 1) % RING) * 2 + core
        seg_far = ((z + 2) % RING) * 2 + core
        seg, top, size, target = (
            (col, 0, half, z_right),
            (col, half, half, z_right),
            (col, half, half, z_left),
            (col, 0, half, z_left),
            (seg_left, 0, half, z_right),
            (seg_right, half, half, z_left),
            (col, 0, segment, twin),
            (seg_left, 0, half, twin),
            (seg_left, half, half, twin),
            (seg_right, half, half, twin),
            (seg_right, 0, half, twin),
            (seg_far, 0, half, twin),
            (seg_far, half, half, twin),
        )[j]
        window = gathered[p].at[pl.ds(seg * per + top // sub, size // sub)]
        sem = N_REDUCE + j
        return pltpu.make_async_remote_copy(
            src_ref=window, dst_ref=window, send_sem=send_sem.at[p, sem], recv_sem=recv_sem.at[p, sem],
            device_id=target, device_id_type=MESH,
        )

    def arrival(p, j):
        seg_left = ((z + 3) % RING) * 2 + core
        seg_right = ((z + 1) % RING) * 2 + core
        seg_far = ((z + 2) % RING) * 2 + core
        flip = 1 - 2 * core
        seg, top, size = (
            (seg_left, 0, half),
            (seg_left, half, half),
            (seg_right, half, half),
            (seg_right, 0, half),
            (seg_far, 0, half),
            (seg_far, half, half),
            (col + flip, 0, segment),
            (seg_left + flip, 0, half),
            (seg_left + flip, half, half),
            (seg_right + flip, half, half),
            (seg_right + flip, 0, half),
            (seg_far + flip, 0, half),
            (seg_far + flip, half, half),
        )[j]
        window = gathered[p].at[pl.ds(seg * per + top // sub, size // sub)]
        sem = N_REDUCE + j
        return pltpu.make_async_remote_copy(
            src_ref=window, dst_ref=window, send_sem=send_sem.at[p, sem], recv_sem=recv_sem.at[p, sem],
            device_id=twin, device_id_type=MESH,
        )

    def reduce_copy(p, i, kind, right, left):
        piece = max(kind - 1, 0)
        rows = (pl.ds(0, half), pl.ds(half, half), pl.ds(0, segment), pl.ds(0, segment))[kind]
        sem = 4 * i + kind
        return pltpu.make_async_remote_copy(
            src_ref=sent.at[p, 3 * i + piece, rows], dst_ref=got.at[p, 3 * i + piece, rows],
            send_sem=send_sem.at[p, sem], recv_sem=recv_sem.at[p, sem],
            device_id=(right, left, right, left)[kind], device_id_type=MESH,
        )

    def start_gather(p):
        for j in (0, 2, 6, 1, 3):
            gather_copy(p, j).start()

    def finish_gather(p):
        arrival(p, 0).wait_recv()
        gather_copy(p, 4).start()
        gather_copy(p, 7).start()
        arrival(p, 2).wait_recv()
        gather_copy(p, 5).start()
        gather_copy(p, 9).start()
        arrival(p, 1).wait_recv()
        gather_copy(p, 8).start()
        arrival(p, 3).wait_recv()
        gather_copy(p, 10).start()
        arrival(p, 4).wait_recv()
        gather_copy(p, 11).start()
        arrival(p, 5).wait_recv()
        gather_copy(p, 12).start()
        for j in range(6, N_GATHER):
            arrival(p, j).wait_recv()

    start_gather(0)

    def sort_group(g, carry):
        keys, first, second = [], 0, 0
        for k in range(slots):
            c = cols_ref[g, k]
            keys.append(c * 8192 + (k * 256 + rows_ref[g, k] * 8 + scale_ref[g, k]))
            first = first + ((2 - c) >> 1)
            second = second + (1 - (c >> 1))
        for i, j in sort_network(slots):
            keys[i], keys[j] = jnp.minimum(keys[i], keys[j]), jnp.maximum(keys[i], keys[j])
        for k in range(slots):
            order[g, k] = ((keys[k] >> 8) & 31) + g * slots
            order[g, slots + k] = (keys[k] >> 3) & 31
            order[g, 2 * slots + k] = keys[k] & 7
        order[g, 3 * slots] = first
        order[g, 3 * slots + 1] = second
        return carry

    lax.fori_loop(0, groups, sort_group, 0)

    def product(p, u, target):
        total = jnp.zeros((tile, classes), F32)
        prefix[u][0] = total
        for q in range(slots):
            source = order[target, slots + q] * (tile // sub)
            labels = jnp.concatenate([gathered[p][source + part] for part in range(tile // sub)], axis=0)
            term = lax.dot_general(tiles[order[target, q]], labels, TN, preferred_element_type=F32)
            total = total + term * order[target, 2 * slots + q].astype(F32)
            prefix[u][q + 1] = total
        one = prefix[u][order[target, 3 * slots]]
        two = prefix[u][order[target, 3 * slots + 1]]
        current[u, 0:tile] = one
        current[u, tile : 2 * tile] = two - one
        current[u, 2 * tile : 3 * tile] = total - two

    upper, lower, whole = pl.ds(0, half), pl.ds(half, half), pl.ds(0, segment)

    def summed(p, i):
        reduce_copy(p, i, 2, a_right, a_left).wait_recv()
        reduce_copy(p, i, 3, a_right, a_left).wait_recv()
        return own[i] + got[p, 3 * i + 1].astype(F32) + got[p, 3 * i + 2].astype(F32)

    for p in range(2):
        finish_gather(p)
        if p == 0:
            for load in loads:
                load.wait()

        def one_step(s, carry):
            far = s < 2
            side = jnp.logical_and(s >= 2, s < 6)
            i0 = jnp.where(far, 2 * s, jnp.where(side, s - 2, 2 * s - 12))
            i1 = jnp.where(side, i0, i0 + 1)
            da0 = jnp.where(far, 2, jnp.where(side, 1, 0))
            da1 = jnp.where(far, 2, jnp.where(side, 3, 0))
            product(p, 0, at(da0, 2 + i0 * (i0 + 1) // 2))
            product(p, 1, at(da1, 2 + i1 * (i1 + 1) // 2))

            @pl.when(far)
            def _():
                for u in range(2):
                    i = 2 * s + u
                    sent[p, 3 * i] = current[u].astype(BF16)
                    reduce_copy(p, i, 0, a_right, a_left).start()
                    reduce_copy(p, i, 1, a_right, a_left).start()

            @pl.when(side)
            def _():
                i = s - 2
                sent[p, 3 * i + 1, half:segment] = current[0, half:segment].astype(BF16)
                sent[p, 3 * i + 2, 0:half] = current[1, 0:half].astype(BF16)
                reduce_copy(p, i, 0, a_right, a_left).wait_recv()
                sent[p, 3 * i + 1, 0:half] = (current[0, 0:half] + got[p, 3 * i, 0:half].astype(F32)).astype(BF16)
                reduce_copy(p, i, 2, a_right, a_left).start()
                reduce_copy(p, i, 1, a_right, a_left).wait_recv()
                sent[p, 3 * i + 2, half:segment] = (
                    current[1, half:segment] + got[p, 3 * i, half:segment].astype(F32)
                ).astype(BF16)
                reduce_copy(p, i, 3, a_right, a_left).start()

            @pl.when(s >= 6)
            def _():
                own[2 * s - 12] = current[0]
                own[2 * s - 11] = current[1]

            @pl.when(s == 6)
            def _():
                sent[p, 12] = summed(p, 0).astype(BF16)
                reduce_copy(p, 4, 0, b_right, b_left).start()
                reduce_copy(p, 4, 1, b_right, b_left).start()

            return carry

        lax.fori_loop(0, 8, one_step, 0)

        total = summed(p, 1)
        reduce_copy(p, 4, 1, b_right, b_left).wait_recv()
        sent[p, 14, 0:half] = total[0:half].astype(BF16)
        sent[p, 14, half:segment] = (total[half:segment] + got[p, 12, half:segment].astype(F32)).astype(BF16)
        reduce_copy(p, 4, 3, b_right, b_left).start()
        total = summed(p, 2)
        reduce_copy(p, 4, 0, b_right, b_left).wait_recv()
        sent[p, 13, half:segment] = total[half:segment].astype(BF16)
        sent[p, 13, 0:half] = (total[0:half] + got[p, 12, 0:half].astype(F32)).astype(BF16)
        reduce_copy(p, 4, 2, b_right, b_left).start()
        own[3] = summed(p, 3)
        reduce_copy(p, 4, 2, b_right, b_left).wait_recv()
        reduce_copy(p, 4, 3, b_right, b_left).wait_recv()
        own[3] = ALPHA * (own[3] + got[p, 13].astype(F32) + got[p, 14].astype(F32))

        if p == 0:
            first = own[3].astype(BF16)
            first_ref[...] = first
            masked = (first.astype(F32) * keep[...]).astype(BF16)
            for part in range(per):
                gathered1[col * per + part] = masked[part * sub : (part + 1) * sub]
            start_gather(1)
        else:
            label_ref[...] = (
                own[3] + (1.0 - ALPHA) * keep[...] * (cot_ref[...].astype(F32) + first_ref[...].astype(F32))
            ).astype(BF16)

    for p in range(2):
        for j in range(N_GATHER):
            gather_copy(p, j).wait_send()
        for i in range(5):
            right, left = (a_right, a_left) if i < 4 else (b_right, b_left)
            for kind in range(4):
                reduce_copy(p, i, kind, right, left).wait_send()


def hand_over(first_in, label_in, first_out, label_out, held, sem):
    loads = [
        pltpu.make_async_copy(first_in, held.at[0], sem.at[0]),
        pltpu.make_async_copy(label_in, held.at[1], sem.at[1]),
    ]
    stores = [
        pltpu.make_async_copy(held.at[0], first_out, sem.at[2]),
        pltpu.make_async_copy(held.at[1], label_out, sem.at[3]),
    ]
    for load in loads:
        load.start()
    for load, store in zip(loads, stores):
        load.wait()
        store.start()
    for store in stores:
        store.wait()


def local(cotangent, seed_label, tile_values, tile_rows, tile_cols, tile_scale):
    segment, classes = cotangent.shape
    _, _, groups, slots, tile, _ = tile_values.shape
    vmem, smem = pl.BlockSpec(memory_space=pltpu.VMEM), pl.BlockSpec(memory_space=pltpu.SMEM)
    out = jax.ShapeDtypeStruct((segment, classes), BF16)
    hbm = pl.BlockSpec(memory_space=pl.ANY)
    results = pl.pallas_call(
        kernel,
        out_shape=(out, out),
        in_specs=[vmem, vmem, smem, smem, smem, pl.BlockSpec(memory_space=pl.ANY)],
        out_specs=(vmem, vmem),
        scratch_shapes=[
            pltpu.VMEM((groups * slots, tile, tile), BF16),
            pltpu.VMEM((2 * RING * segment // 64, 64, classes), BF16),
            pltpu.VMEM((2 * RING * segment // 64, 64, classes), BF16),
            pltpu.VMEM((slots + 1, tile, classes), F32),
            pltpu.VMEM((slots + 1, tile, classes), F32),
            pltpu.VMEM((2, segment, classes), F32),
            pltpu.VMEM((4, segment, classes), F32),
            pltpu.VMEM((2, 15, segment, classes), BF16),
            pltpu.VMEM((2, 15, segment, classes), BF16),
            pltpu.VMEM((segment, classes), F32),
            pltpu.SMEM((groups, 3 * slots + 2), jnp.int32),
            pltpu.SemaphoreType.DMA((4,)),
            pltpu.SemaphoreType.DMA((2, N_REDUCE + N_GATHER)),
            pltpu.SemaphoreType.DMA((2, N_REDUCE + N_GATHER)),
        ],
        compiler_params=pltpu.CompilerParams(
            collective_id=0, has_side_effects=True, vmem_limit_bytes=56 * 1024 * 1024
        ),
        name="propagate_twice",
    )(
        cotangent,
        seed_label.reshape(segment // tile, tile),
        tile_rows[0, 0],
        tile_cols[0, 0],
        tile_scale[0, 0],
        tile_values.reshape(groups * slots, tile, tile),
    )
    return pl.pallas_call(
        hand_over,
        out_shape=(out, out),
        in_specs=[hbm, hbm],
        out_specs=(hbm, hbm),
        scratch_shapes=[pltpu.VMEM((2, segment, classes), BF16), pltpu.SemaphoreType.DMA((4,))],
        name="finish_results",
    )(*results)


def solution(mesh):
    return jax.shard_map(
        local,
        mesh=mesh,
        in_specs=(
            P(("row", "col"), None),
            P(("row", "col")),
            P("row", "col", None, None, None, None),
            P("row", "col", None, None),
            P("row", "col", None, None),
            P("row", "col", None, None),
        ),
        out_specs=(P(("row", "col"), None), P(("row", "col"), None)),
        check_vma=False,
    )
```

```python
import jax
import jax.numpy as jnp
from jax import lax
from jax.experimental import pallas as pl
from jax.experimental.pallas import tpu as pltpu
from jax.sharding import PartitionSpec as P

ALPHA = 0.9
MESH = pl.DeviceIdType.MESH
F32 = jnp.float32
BF16 = jnp.bfloat16
RING = 4
TN = (((0,), (0,)), ((), ()))
N_REDUCE = 30
N_GATHER = 13


def sort_network(count):
    size = 1
    while size < count:
        size *= 2
    pairs = []
    p = 1
    while p < size:
        k = p
        while k >= 1:
            for j in range(k % p, size - k, 2 * k):
                for i in range(min(k, size - j - k)):
                    if (i + j) // (p * 2) == (i + j + k) // (p * 2) and i + j + k < count:
                        pairs.append((i + j, i + j + k))
            k //= 2
        p *= 2
    return pairs


def kernel(
    cot_hbm, seed_hbm, rows_hbm, cols_hbm, scale_hbm, tiles_hbm,
    first_ref, label_ref,
    cot_ref, seed_ref, rows_ref, cols_ref, scale_ref, small_sem, tiles, gathered0, gathered1, prefix0, prefix1, current, own, sent, got, keep, order,
    tile_sem, send_sem, recv_sem,
):
    tile = tiles.shape[1]
    groups = rows_ref.shape[0]
    slots = tiles.shape[0] // groups
    gathered = (gathered0, gathered1)
    prefix = (prefix0, prefix1)
    sub = gathered0.shape[1]
    segment, classes = cot_ref.shape
    half = segment // 2
    per = segment // sub
    row, col = lax.axis_index("row"), lax.axis_index("col")
    y, x = row // RING, row % RING
    z, core = col // 2, col % 2
    a = x + core * (y - x)
    b = y + core * (x - y)
    step_a = 1 + 3 * core
    step_b = 4 - 3 * core

    def at(da, db):
        return ((a + da) % RING) * step_a + ((b + db) % RING) * step_b

    def device(da, db):
        return {"row": at(da, db), "col": col}

    a_right, a_left = device(1, 0), device(3, 0)
    b_right, b_left = device(0, 1), device(0, 3)
    z_right = {"row": row, "col": ((z + 1) % RING) * 2 + core}
    z_left = {"row": row, "col": ((z + 3) % RING) * 2 + core}
    twin = {"row": row, "col": z * 2 + (1 - core)}

    barrier = pltpu.get_barrier_semaphore()
    for other in (a_right, a_left, b_right, b_left, z_right, z_left, twin):
        pl.semaphore_signal(barrier, inc=1, device_id=other, device_id_type=MESH)

    small = [
        pltpu.make_async_copy(source, target, small_sem.at[q])
        for q, (source, target) in enumerate((
            (cot_hbm, cot_ref), (seed_hbm, seed_ref), (rows_hbm, rows_ref), (cols_hbm, cols_ref), (scale_hbm, scale_ref)
        ))
    ]
    for load in small:
        load.start()
    loads = [
        pltpu.make_async_copy(
            tiles_hbm.at[pl.ds(q * tiles.shape[0] // 4, tiles.shape[0] // 4)],
            tiles.at[pl.ds(q * tiles.shape[0] // 4, tiles.shape[0] // 4)],
            tile_sem.at[q],
        )
        for q in range(4)
    ]
    for load in loads:
        load.start()

    small[0].wait()
    small[1].wait()
    for block in range(segment // tile):
        seeds = jnp.broadcast_to(seed_ref[block : block + 1, :], (tile, tile)).T
        lanes = lax.broadcasted_iota(jnp.int32, (tile, tile), 1)
        rows = slice(block * tile, (block + 1) * tile)
        for c in range(classes // tile):
            lane = slice(c * tile, (c + 1) * tile)
            kept = jnp.where(seeds == lanes + c * tile, 0.0, 1.0)
            keep[rows, lane] = kept
            masked = (cot_ref[rows, lane].astype(F32) * kept).astype(BF16)
            for part in range(tile // sub):
                gathered0[col * per + block * (tile // sub) + part, :, lane] = masked[part * sub : (part + 1) * sub]

    pl.semaphore_wait(barrier, 7)

    def gather_copy(p, j):
        seg_left = ((z + 3) % RING) * 2 + core
        seg_right = ((z + 1) % RING) * 2 + core
        seg_far = ((z + 2) % RING) * 2 + core
        seg, top, size, target = (
            (col, 0, half, z_right),
            (col, half, half, z_right),
            (col, half, half, z_left),
            (col, 0, half, z_left),
            (seg_left, 0, half, z_right),
            (seg_right, half, half, z_left),
            (col, 0, segment, twin),
            (seg_left, 0, half, twin),
            (seg_left, half, half, twin),
            (seg_right, half, half, twin),
            (seg_right, 0, half, twin),
            (seg_far, 0, half, twin),
            (seg_far, half, half, twin),
        )[j]
        window = gathered[p].at[pl.ds(seg * per + top // sub, size // sub)]
        sem = N_REDUCE + j
        return pltpu.make_async_remote_copy(
            src_ref=window, dst_ref=window, send_sem=send_sem.at[p, sem], recv_sem=recv_sem.at[p, sem],
            device_id=target, device_id_type=MESH,
        )

    def arrival(p, j):
        seg_left = ((z + 3) % RING) * 2 + core
        seg_right = ((z + 1) % RING) * 2 + core
        seg_far = ((z + 2) % RING) * 2 + core
        flip = 1 - 2 * core
        seg, top, size = (
            (seg_left, 0, half),
            (seg_left, half, half),
            (seg_right, half, half),
            (seg_right, 0, half),
            (seg_far, 0, half),
            (seg_far, half, half),
            (col + flip, 0, segment),
            (seg_left + flip, 0, half),
            (seg_left + flip, half, half),
            (seg_right + flip, half, half),
            (seg_right + flip, 0, half),
            (seg_far + flip, 0, half),
            (seg_far + flip, half, half),
        )[j]
        window = gathered[p].at[pl.ds(seg * per + top // sub, size // sub)]
        sem = N_REDUCE + j
        return pltpu.make_async_remote_copy(
            src_ref=window, dst_ref=window, send_sem=send_sem.at[p, sem], recv_sem=recv_sem.at[p, sem],
            device_id=twin, device_id_type=MESH,
        )

    upper, lower = pl.ds(0, half), pl.ds(half, half)

    def reduce_copy(p, i, kind, right, left):
        piece = 3 * i + kind // 2
        rows = (upper, lower, upper, lower, lower, upper)[kind]
        sem = 6 * i + kind
        return pltpu.make_async_remote_copy(
            src_ref=sent.at[p, piece, rows], dst_ref=got.at[p, piece, rows],
            send_sem=send_sem.at[p, sem], recv_sem=recv_sem.at[p, sem],
            device_id=(right, left, right, right, left, left)[kind], device_id_type=MESH,
        )

    def along_a(p, i, kind):
        return reduce_copy(p, i, kind, a_right, a_left)

    def along_b(p, kind):
        return reduce_copy(p, 4, kind, b_right, b_left)

    def start_gather(p):
        for j in (0, 2, 6, 1, 3):
            gather_copy(p, j).start()

    def finish_gather(p):
        arrival(p, 0).wait_recv()
        gather_copy(p, 4).start()
        gather_copy(p, 7).start()
        arrival(p, 2).wait_recv()
        gather_copy(p, 5).start()
        gather_copy(p, 9).start()
        arrival(p, 1).wait_recv()
        gather_copy(p, 8).start()
        arrival(p, 3).wait_recv()
        gather_copy(p, 10).start()
        arrival(p, 4).wait_recv()
        gather_copy(p, 11).start()
        arrival(p, 5).wait_recv()
        gather_copy(p, 12).start()
        for j in range(6, N_GATHER):
            arrival(p, j).wait_recv()

    start_gather(0)

    for load in small[2:]:
        load.wait()

    def sort_group(g, carry):
        keys, first, second = [], 0, 0
        for k in range(slots):
            c = cols_ref[g, k]
            keys.append(c * 8192 + (k * 256 + rows_ref[g, k] * 8 + scale_ref[g, k]))
            first = first + ((2 - c) >> 1)
            second = second + (1 - (c >> 1))
        for i, j in sort_network(slots):
            keys[i], keys[j] = jnp.minimum(keys[i], keys[j]), jnp.maximum(keys[i], keys[j])
        for k in range(slots):
            order[g, k] = ((keys[k] >> 8) & 31) + g * slots
            order[g, slots + k] = (keys[k] >> 3) & 31
            order[g, 2 * slots + k] = keys[k] & 7
        order[g, 3 * slots] = first
        order[g, 3 * slots + 1] = second
        return carry

    lax.fori_loop(0, groups, sort_group, 0)

    def product(p, u, target):
        total = jnp.zeros((tile, classes), F32)
        prefix[u][0] = total
        for q in range(slots):
            source = order[target, slots + q] * (tile // sub)
            labels = jnp.concatenate([gathered[p][source + part] for part in range(tile // sub)], axis=0)
            term = lax.dot_general(tiles[order[target, q]], labels, TN, preferred_element_type=F32)
            total = total + term * order[target, 2 * slots + q].astype(F32)
            prefix[u][q + 1] = total
        one = prefix[u][order[target, 3 * slots]]
        two = prefix[u][order[target, 3 * slots + 1]]
        current[u, 0:tile] = one
        current[u, tile : 2 * tile] = two - one
        current[u, 2 * tile : 3 * tile] = total - two

    def summed(p, i, rows, from_left, from_right):
        along_a(p, i, from_left).wait_recv()
        along_a(p, i, from_right).wait_recv()
        return own[i, rows] + got[p, 3 * i + 1, rows].astype(F32) + got[p, 3 * i + 2, rows].astype(F32)

    for p in range(2):
        finish_gather(p)
        if p == 0:
            for load in loads:
                load.wait()

        def one_step(s, carry):
            far = s < 2
            side = jnp.logical_and(s >= 2, s < 6)
            i0 = jnp.where(far, 2 * s, jnp.where(side, s - 2, 2 * s - 12))
            i1 = jnp.where(side, i0, i0 + 1)
            da0 = jnp.where(far, 2, jnp.where(side, 1, 0))
            da1 = jnp.where(far, 2, jnp.where(side, 3, 0))
            product(p, 0, at(da0, 2 + i0 * (i0 + 1) // 2))
            product(p, 1, at(da1, 2 + i1 * (i1 + 1) // 2))

            @pl.when(far)
            def _():
                for u in range(2):
                    i = 2 * s + u
                    sent[p, 3 * i] = current[u].astype(BF16)
                    along_a(p, i, 0).start()
                    along_a(p, i, 1).start()

            @pl.when(side)
            def _():
                i = s - 2
                sent[p, 3 * i + 1, half:segment] = current[0, half:segment].astype(BF16)
                along_a(p, i, 3).start()
                sent[p, 3 * i + 2, 0:half] = current[1, 0:half].astype(BF16)
                along_a(p, i, 5).start()
                along_a(p, i, 0).wait_recv()
                sent[p, 3 * i + 1, 0:half] = (current[0, 0:half] + got[p, 3 * i, 0:half].astype(F32)).astype(BF16)
                along_a(p, i, 2).start()
                along_a(p, i, 1).wait_recv()
                sent[p, 3 * i + 2, half:segment] = (
                    current[1, half:segment] + got[p, 3 * i, half:segment].astype(F32)
                ).astype(BF16)
                along_a(p, i, 4).start()

            @pl.when(s >= 6)
            def _():
                own[2 * s - 12] = current[0]
                own[2 * s - 11] = current[1]

            @pl.when(s == 6)
            def _():
                sent[p, 12, upper] = summed(p, 0, upper, 2, 5).astype(BF16)
                along_b(p, 0).start()
                sent[p, 12, lower] = summed(p, 0, lower, 3, 4).astype(BF16)
                along_b(p, 1).start()

            return carry

        lax.fori_loop(0, 8, one_step, 0)

        sent[p, 14, upper] = summed(p, 1, upper, 2, 5).astype(BF16)
        along_b(p, 5).start()
        sent[p, 13, lower] = summed(p, 2, lower, 3, 4).astype(BF16)
        along_b(p, 3).start()
        total = summed(p, 1, lower, 3, 4)
        along_b(p, 1).wait_recv()
        sent[p, 14, lower] = (total + got[p, 12, lower].astype(F32)).astype(BF16)
        along_b(p, 4).start()
        total = summed(p, 2, upper, 2, 5)
        along_b(p, 0).wait_recv()
        sent[p, 13, upper] = (total + got[p, 12, upper].astype(F32)).astype(BF16)
        along_b(p, 2).start()
        own[3, upper] = summed(p, 3, upper, 2, 5)
        own[3, lower] = summed(p, 3, lower, 3, 4)
        for top, from_left, from_right in ((0, 2, 5), (half, 3, 4)):
            rows = pl.ds(top, half)
            along_b(p, from_left).wait_recv()
            along_b(p, from_right).wait_recv()
            total = ALPHA * (own[3, rows] + got[p, 13, rows].astype(F32) + got[p, 14, rows].astype(F32))
            if p == 0:
                first = total.astype(BF16)
                masked = (first.astype(F32) * keep[rows]).astype(BF16)
                for part in range(half // sub):
                    gathered1[col * per + top // sub + part] = masked[part * sub : (part + 1) * sub]
                for j in (0,) if top == 0 else (2, 6, 1, 3):
                    gather_copy(1, j).start()
                first_ref[rows] = first
            else:
                label_ref[rows] = (
                    total + (1.0 - ALPHA) * keep[rows] * (cot_ref[rows].astype(F32) + first_ref[rows].astype(F32))
                ).astype(BF16)

    for p in range(2):
        for j in range(N_GATHER):
            gather_copy(p, j).wait_send()
        for kind in range(6):
            for i in range(4):
                along_a(p, i, kind).wait_send()
            along_b(p, kind).wait_send()


def hand_over(first_in, label_in, first_out, label_out):
    first_out[...] = first_in[...]
    label_out[...] = label_in[...]


def local(cotangent, seed_label, tile_values, tile_rows, tile_cols, tile_scale):
    segment, classes = cotangent.shape
    _, _, groups, slots, tile, _ = tile_values.shape
    vmem = pl.BlockSpec(memory_space=pltpu.VMEM)
    out = jax.ShapeDtypeStruct((segment, classes), BF16)
    results = pl.pallas_call(
        kernel,
        out_shape=(out, out),
        in_specs=[pl.BlockSpec(memory_space=pltpu.HBM)] * 6,
        out_specs=(vmem, vmem),
        scratch_shapes=[
            pltpu.VMEM((segment, classes), BF16),
            pltpu.VMEM((segment // tile, tile), jnp.int32),
            pltpu.SMEM((groups, slots), jnp.int32),
            pltpu.SMEM((groups, slots), jnp.int32),
            pltpu.SMEM((groups, slots), jnp.int32),
            pltpu.SemaphoreType.DMA((5,)),
            pltpu.VMEM((groups * slots, tile, tile), BF16),
            pltpu.VMEM((2 * RING * segment // 64, 64, classes), BF16),
            pltpu.VMEM((2 * RING * segment // 64, 64, classes), BF16),
            pltpu.VMEM((slots + 1, tile, classes), F32),
            pltpu.VMEM((slots + 1, tile, classes), F32),
            pltpu.VMEM((2, segment, classes), F32),
            pltpu.VMEM((4, segment, classes), F32),
            pltpu.VMEM((2, 15, segment, classes), BF16),
            pltpu.VMEM((2, 15, segment, classes), BF16),
            pltpu.VMEM((segment, classes), F32),
            pltpu.SMEM((groups, 3 * slots + 2), jnp.int32),
            pltpu.SemaphoreType.DMA((4,)),
            pltpu.SemaphoreType.DMA((2, N_REDUCE + N_GATHER)),
            pltpu.SemaphoreType.DMA((2, N_REDUCE + N_GATHER)),
        ],
        compiler_params=pltpu.CompilerParams(
            collective_id=0, has_side_effects=True, vmem_limit_bytes=42 * 1024 * 1024
        ),
        name="propagate_twice",
    )(
        pltpu.with_memory_space_constraint(cotangent, pltpu.HBM),
        pltpu.with_memory_space_constraint(seed_label.reshape(segment // tile, tile), pltpu.HBM),
        pltpu.with_memory_space_constraint(tile_rows[0, 0], pltpu.HBM),
        pltpu.with_memory_space_constraint(tile_cols[0, 0], pltpu.HBM),
        pltpu.with_memory_space_constraint(tile_scale[0, 0], pltpu.HBM),
        tile_values.reshape(groups * slots, tile, tile),
    )
    return pl.pallas_call(
        hand_over,
        out_shape=(out, out),
        in_specs=[vmem, vmem],
        out_specs=(vmem, vmem),
        compiler_params=pltpu.CompilerParams(vmem_limit_bytes=4 * 1024 * 1024),
        name="finish_results",
    )(*results)


def solution(mesh):
    return jax.shard_map(
        local,
        mesh=mesh,
        in_specs=(
            P(("row", "col"), None),
            P(("row", "col")),
            P("row", "col", None, None, None, None),
            P("row", "col", None, None),
            P("row", "col", None, None),
            P("row", "col", None, None),
        ),
        out_specs=(P(("row", "col"), None), P(("row", "col"), None)),
        check_vma=False,
    )
```

```python
import jax
import jax.numpy as jnp
from jax import lax
from jax.experimental import pallas as pl
from jax.experimental.pallas import tpu as pltpu
from jax.sharding import PartitionSpec as P

ALPHA = 0.9
MESH = pl.DeviceIdType.MESH
F32 = jnp.float32
BF16 = jnp.bfloat16
RING = 4
TN = (((0,), (0,)), ((), ()))
N_REDUCE = 30
N_GATHER = 13


def sort_network(count):
    size = 1
    while size < count:
        size *= 2
    pairs = []
    p = 1
    while p < size:
        k = p
        while k >= 1:
            for j in range(k % p, size - k, 2 * k):
                for i in range(min(k, size - j - k)):
                    if (i + j) // (p * 2) == (i + j + k) // (p * 2) and i + j + k < count:
                        pairs.append((i + j, i + j + k))
            k //= 2
        p *= 2
    return pairs


def kernel(
    cot_hbm, seed_hbm, rows_hbm, cols_hbm, scale_hbm, tiles_hbm,
    first_ref, label_ref,
    cot_ref, seed_ref, rows_ref, cols_ref, scale_ref, small_sem, tiles, gathered0, gathered1, prefix0, prefix1, current, own, sent, got, keep, order,
    tile_sem, send_sem, recv_sem,
):
    tile = tiles.shape[1]
    groups = rows_ref.shape[0]
    slots = tiles.shape[0] // groups
    gathered = (gathered0, gathered1)
    prefix = (prefix0, prefix1)
    sub = gathered0.shape[1]
    segment, classes = cot_ref.shape
    half = segment // 2
    per = segment // sub
    row, col = lax.axis_index("row"), lax.axis_index("col")
    y, x = row // RING, row % RING
    z, core = col // 2, col % 2
    a = x + core * (y - x)
    b = y + core * (x - y)
    step_a = 1 + 3 * core
    step_b = 4 - 3 * core

    def at(da, db):
        return ((a + da) % RING) * step_a + ((b + db) % RING) * step_b

    def device(da, db):
        return {"row": at(da, db), "col": col}

    a_right, a_left = device(1, 0), device(3, 0)
    b_right, b_left = device(0, 1), device(0, 3)
    z_right = {"row": row, "col": ((z + 1) % RING) * 2 + core}
    z_left = {"row": row, "col": ((z + 3) % RING) * 2 + core}
    twin = {"row": row, "col": z * 2 + (1 - core)}

    barrier = pltpu.get_barrier_semaphore()
    for other in (a_right, a_left, b_right, b_left, z_right, z_left, twin):
        pl.semaphore_signal(barrier, inc=1, device_id=other, device_id_type=MESH)

    small = [
        pltpu.make_async_copy(source, target, small_sem.at[q])
        for q, (source, target) in enumerate((
            (cot_hbm, cot_ref), (seed_hbm, seed_ref), (rows_hbm, rows_ref), (cols_hbm, cols_ref), (scale_hbm, scale_ref)
        ))
    ]
    for load in small:
        load.start()
    loads = [
        pltpu.make_async_copy(
            tiles_hbm.at[pl.ds(q * tiles.shape[0] // 4, tiles.shape[0] // 4)],
            tiles.at[pl.ds(q * tiles.shape[0] // 4, tiles.shape[0] // 4)],
            tile_sem.at[q],
        )
        for q in range(4)
    ]
    for load in loads:
        load.start()

    small[0].wait()
    small[1].wait()
    for block in range(segment // tile):
        seeds = jnp.broadcast_to(seed_ref[block : block + 1, :], (tile, tile)).T
        lanes = lax.broadcasted_iota(jnp.int32, (tile, tile), 1)
        rows = slice(block * tile, (block + 1) * tile)
        for c in range(classes // tile):
            lane = slice(c * tile, (c + 1) * tile)
            kept = jnp.where(seeds == lanes + c * tile, 0.0, 1.0)
            keep[rows, lane] = kept
            masked = (cot_ref[rows, lane].astype(F32) * kept).astype(BF16)
            for part in range(tile // sub):
                gathered0[col * per + block * (tile // sub) + part, :, lane] = masked[part * sub : (part + 1) * sub]

    pl.semaphore_wait(barrier, 7)

    def gather_copy(p, j):
        seg_left = ((z + 3) % RING) * 2 + core
        seg_right = ((z + 1) % RING) * 2 + core
        seg_far = ((z + 2) % RING) * 2 + core
        seg, top, size, target = (
            (col, 0, half, z_right),
            (col, half, half, z_right),
            (col, half, half, z_left),
            (col, 0, half, z_left),
            (seg_left, 0, half, z_right),
            (seg_right, half, half, z_left),
            (col, 0, segment, twin),
            (seg_left, 0, half, twin),
            (seg_left, half, half, twin),
            (seg_right, half, half, twin),
            (seg_right, 0, half, twin),
            (seg_far, 0, half, twin),
            (seg_far, half, half, twin),
        )[j]
        window = gathered[p].at[pl.ds(seg * per + top // sub, size // sub)]
        sem = N_REDUCE + j
        return pltpu.make_async_remote_copy(
            src_ref=window, dst_ref=window, send_sem=send_sem.at[p, sem], recv_sem=recv_sem.at[p, sem],
            device_id=target, device_id_type=MESH,
        )

    def arrival(p, j):
        seg_left = ((z + 3) % RING) * 2 + core
        seg_right = ((z + 1) % RING) * 2 + core
        seg_far = ((z + 2) % RING) * 2 + core
        flip = 1 - 2 * core
        seg, top, size = (
            (seg_left, 0, half),
            (seg_left, half, half),
            (seg_right, half, half),
            (seg_right, 0, half),
            (seg_far, 0, half),
            (seg_far, half, half),
            (col + flip, 0, segment),
            (seg_left + flip, 0, half),
            (seg_left + flip, half, half),
            (seg_right + flip, half, half),
            (seg_right + flip, 0, half),
            (seg_far + flip, 0, half),
            (seg_far + flip, half, half),
        )[j]
        window = gathered[p].at[pl.ds(seg * per + top // sub, size // sub)]
        sem = N_REDUCE + j
        return pltpu.make_async_remote_copy(
            src_ref=window, dst_ref=window, send_sem=send_sem.at[p, sem], recv_sem=recv_sem.at[p, sem],
            device_id=twin, device_id_type=MESH,
        )

    upper, lower = pl.ds(0, half), pl.ds(half, half)

    def reduce_copy(p, i, kind, right, left):
        piece = 3 * i + kind // 2
        rows = (upper, lower, upper, lower, lower, upper)[kind]
        sem = 6 * i + kind
        return pltpu.make_async_remote_copy(
            src_ref=sent.at[p, piece, rows], dst_ref=got.at[p, piece, rows],
            send_sem=send_sem.at[p, sem], recv_sem=recv_sem.at[p, sem],
            device_id=(right, left, right, right, left, left)[kind], device_id_type=MESH,
        )

    def along_a(p, i, kind):
        return reduce_copy(p, i, kind, a_right, a_left)

    def along_b(p, kind):
        return reduce_copy(p, 4, kind, b_right, b_left)

    def start_gather(p):
        for j in (0, 2, 6, 1, 3):
            gather_copy(p, j).start()

    def finish_gather(p):
        arrival(p, 0).wait_recv()
        gather_copy(p, 4).start()
        gather_copy(p, 7).start()
        arrival(p, 2).wait_recv()
        gather_copy(p, 5).start()
        gather_copy(p, 9).start()
        arrival(p, 1).wait_recv()
        gather_copy(p, 8).start()
        arrival(p, 3).wait_recv()
        gather_copy(p, 10).start()
        arrival(p, 4).wait_recv()
        gather_copy(p, 11).start()
        arrival(p, 5).wait_recv()
        gather_copy(p, 12).start()
        for j in range(6, N_GATHER):
            arrival(p, j).wait_recv()

    start_gather(0)

    for load in small[2:]:
        load.wait()

    def sort_group(g, carry):
        keys, first, second = [], 0, 0
        for k in range(slots):
            c = cols_ref[g, k]
            keys.append(c * 8192 + (k * 256 + rows_ref[g, k] * 8 + scale_ref[g, k]))
            first = first + ((2 - c) >> 1)
            second = second + (1 - (c >> 1))
        for i, j in sort_network(slots):
            keys[i], keys[j] = jnp.minimum(keys[i], keys[j]), jnp.maximum(keys[i], keys[j])
        for k in range(slots):
            order[g, k] = ((keys[k] >> 8) & 31) + g * slots
            order[g, slots + k] = (keys[k] >> 3) & 31
            order[g, 2 * slots + k] = keys[k] & 7
        order[g, 3 * slots] = first
        order[g, 3 * slots + 1] = second
        return carry

    lax.fori_loop(0, groups, sort_group, 0)

    def product(p, u, target):
        total = jnp.zeros((tile, classes), F32)
        prefix[u][0] = total
        for q in range(slots):
            source = order[target, slots + q] * (tile // sub)
            labels = jnp.concatenate([gathered[p][source + part] for part in range(tile // sub)], axis=0)
            term = lax.dot_general(tiles[order[target, q]], labels, TN, preferred_element_type=F32)
            total = total + term * order[target, 2 * slots + q].astype(F32)
            prefix[u][q + 1] = total
        one = prefix[u][order[target, 3 * slots]]
        two = prefix[u][order[target, 3 * slots + 1]]
        current[u, 0:tile] = one
        current[u, tile : 2 * tile] = two - one
        current[u, 2 * tile : 3 * tile] = total - two

    def summed(p, i, rows, from_left, from_right):
        along_a(p, i, from_left).wait_recv()
        along_a(p, i, from_right).wait_recv()
        return own[i, rows] + got[p, 3 * i + 1, rows].astype(F32) + got[p, 3 * i + 2, rows].astype(F32)

    for p in range(2):
        finish_gather(p)
        if p == 0:
            for load in loads:
                load.wait()

        def send_whole(u, i):
            sent[p, 3 * i] = current[u].astype(BF16)
            along_a(p, i, 0).start()
            along_a(p, i, 1).start()

        for i in range(2):
            product(p, i, at(2, 2 + i * (i + 1) // 2))
            send_whole(i, i)

        def one_step(s, carry):
            far = s < 2
            side = jnp.logical_and(s >= 2, s < 6)
            i0 = jnp.where(far, 2 * s, jnp.where(side, s - 2, 2 * s - 12))
            i1 = jnp.where(side, i0, i0 + 1)
            da0 = jnp.where(far, 2, jnp.where(side, 1, 0))
            da1 = jnp.where(far, 2, jnp.where(side, 3, 0))
            product(p, 0, at(da0, 2 + i0 * (i0 + 1) // 2))
            product(p, 1, at(da1, 2 + i1 * (i1 + 1) // 2))

            @pl.when(far)
            def _():
                for u in range(2):
                    send_whole(u, 2 * s + u)

            @pl.when(side)
            def _():
                i = s - 2
                sent[p, 3 * i + 1, half:segment] = current[0, half:segment].astype(BF16)
                along_a(p, i, 3).start()
                sent[p, 3 * i + 2, 0:half] = current[1, 0:half].astype(BF16)
                along_a(p, i, 5).start()
                along_a(p, i, 0).wait_recv()
                sent[p, 3 * i + 1, 0:half] = (current[0, 0:half] + got[p, 3 * i, 0:half].astype(F32)).astype(BF16)
                along_a(p, i, 2).start()
                along_a(p, i, 1).wait_recv()
                sent[p, 3 * i + 2, half:segment] = (
                    current[1, half:segment] + got[p, 3 * i, half:segment].astype(F32)
                ).astype(BF16)
                along_a(p, i, 4).start()

            @pl.when(s >= 6)
            def _():
                own[2 * s - 12] = current[0]
                own[2 * s - 11] = current[1]

            @pl.when(s == 6)
            def _():
                sent[p, 12, upper] = summed(p, 0, upper, 2, 5).astype(BF16)
                along_b(p, 0).start()
                sent[p, 12, lower] = summed(p, 0, lower, 3, 4).astype(BF16)
                along_b(p, 1).start()

            return carry

        lax.fori_loop(1, 8, one_step, 0)

        sent[p, 14, upper] = summed(p, 1, upper, 2, 5).astype(BF16)
        along_b(p, 5).start()
        sent[p, 13, lower] = summed(p, 2, lower, 3, 4).astype(BF16)
        along_b(p, 3).start()
        total = summed(p, 1, lower, 3, 4)
        along_b(p, 1).wait_recv()
        sent[p, 14, lower] = (total + got[p, 12, lower].astype(F32)).astype(BF16)
        along_b(p, 4).start()
        total = summed(p, 2, upper, 2, 5)
        along_b(p, 0).wait_recv()
        sent[p, 13, upper] = (total + got[p, 12, upper].astype(F32)).astype(BF16)
        along_b(p, 2).start()
        own[3, upper] = summed(p, 3, upper, 2, 5)
        own[3, lower] = summed(p, 3, lower, 3, 4)
        for top, from_left, from_right in ((0, 2, 5), (half, 3, 4)):
            rows = pl.ds(top, half)
            along_b(p, from_left).wait_recv()
            along_b(p, from_right).wait_recv()
            total = ALPHA * (own[3, rows] + got[p, 13, rows].astype(F32) + got[p, 14, rows].astype(F32))
            if p == 0:
                first = total.astype(BF16)
                masked = (first.astype(F32) * keep[rows]).astype(BF16)
                for part in range(half // sub):
                    gathered1[col * per + top // sub + part] = masked[part * sub : (part + 1) * sub]
                for j in (0,) if top == 0 else (2, 6, 1, 3):
                    gather_copy(1, j).start()
                first_ref[rows] = first
            else:
                label_ref[rows] = (
                    total + (1.0 - ALPHA) * keep[rows] * (cot_ref[rows].astype(F32) + first_ref[rows].astype(F32))
                ).astype(BF16)

    for p in range(2):
        for j in range(N_GATHER):
            gather_copy(p, j).wait_send()
        for kind in range(6):
            for i in range(4):
                along_a(p, i, kind).wait_send()
            along_b(p, kind).wait_send()


def hand_over(first_in, label_in, first_out, label_out):
    first_out[...] = first_in[...]
    label_out[...] = label_in[...]


def local(cotangent, seed_label, tile_values, tile_rows, tile_cols, tile_scale):
    segment, classes = cotangent.shape
    _, _, groups, slots, tile, _ = tile_values.shape
    vmem = pl.BlockSpec(memory_space=pltpu.VMEM)
    out = jax.ShapeDtypeStruct((segment, classes), BF16)
    results = pl.pallas_call(
        kernel,
        out_shape=(out, out),
        in_specs=[pl.BlockSpec(memory_space=pltpu.HBM)] * 6,
        out_specs=(vmem, vmem),
        scratch_shapes=[
            pltpu.VMEM((segment, classes), BF16),
            pltpu.VMEM((segment // tile, tile), jnp.int32),
            pltpu.SMEM((groups, slots), jnp.int32),
            pltpu.SMEM((groups, slots), jnp.int32),
            pltpu.SMEM((groups, slots), jnp.int32),
            pltpu.SemaphoreType.DMA((5,)),
            pltpu.VMEM((groups * slots, tile, tile), BF16),
            pltpu.VMEM((2 * RING * segment // 64, 64, classes), BF16),
            pltpu.VMEM((2 * RING * segment // 64, 64, classes), BF16),
            pltpu.VMEM((slots + 1, tile, classes), F32),
            pltpu.VMEM((slots + 1, tile, classes), F32),
            pltpu.VMEM((2, segment, classes), F32),
            pltpu.VMEM((4, segment, classes), F32),
            pltpu.VMEM((2, 15, segment, classes), BF16),
            pltpu.VMEM((2, 15, segment, classes), BF16),
            pltpu.VMEM((segment, classes), F32),
            pltpu.SMEM((groups, 3 * slots + 2), jnp.int32),
            pltpu.SemaphoreType.DMA((4,)),
            pltpu.SemaphoreType.DMA((2, N_REDUCE + N_GATHER)),
            pltpu.SemaphoreType.DMA((2, N_REDUCE + N_GATHER)),
        ],
        compiler_params=pltpu.CompilerParams(
            collective_id=0, has_side_effects=True, vmem_limit_bytes=42 * 1024 * 1024
        ),
        name="propagate_twice",
    )(
        pltpu.with_memory_space_constraint(cotangent, pltpu.HBM),
        pltpu.with_memory_space_constraint(seed_label.reshape(segment // tile, tile), pltpu.HBM),
        pltpu.with_memory_space_constraint(tile_rows[0, 0], pltpu.HBM),
        pltpu.with_memory_space_constraint(tile_cols[0, 0], pltpu.HBM),
        pltpu.with_memory_space_constraint(tile_scale[0, 0], pltpu.HBM),
        tile_values.reshape(groups * slots, tile, tile),
    )
    return pl.pallas_call(
        hand_over,
        out_shape=(out, out),
        in_specs=[vmem, vmem],
        out_specs=(vmem, vmem),
        compiler_params=pltpu.CompilerParams(vmem_limit_bytes=4 * 1024 * 1024),
        name="finish_results",
    )(*results)


def solution(mesh):
    return jax.shard_map(
        local,
        mesh=mesh,
        in_specs=(
            P(("row", "col"), None),
            P(("row", "col")),
            P("row", "col", None, None, None, None),
            P("row", "col", None, None),
            P("row", "col", None, None),
            P("row", "col", None, None),
        ),
        out_specs=(P(("row", "col"), None), P(("row", "col"), None)),
        check_vma=False,
    )
```

```python
import jax
import jax.numpy as jnp
from jax import lax
from jax.experimental import pallas as pl
from jax.experimental.pallas import tpu as pltpu
from jax.sharding import PartitionSpec as P

ALPHA = 0.9
MESH = pl.DeviceIdType.MESH
F32 = jnp.float32
BF16 = jnp.bfloat16
RING = 4
TN = (((0,), (0,)), ((), ()))
N_REDUCE = 30
N_GATHER = 13


def sort_network(count):
    size = 1
    while size < count:
        size *= 2
    pairs = []
    p = 1
    while p < size:
        k = p
        while k >= 1:
            for j in range(k % p, size - k, 2 * k):
                for i in range(min(k, size - j - k)):
                    if (i + j) // (p * 2) == (i + j + k) // (p * 2) and i + j + k < count:
                        pairs.append((i + j, i + j + k))
            k //= 2
        p *= 2
    return pairs


def kernel(
    cot_hbm, seed_hbm, rows_hbm, cols_hbm, scale_hbm, tiles_hbm,
    first_ref, label_ref,
    cot_ref, seed_ref, rows_ref, cols_ref, scale_ref, small_sem, tiles, gathered0, gathered1, prefix0, prefix1, current, own, sent, got, keep, order,
    tile_sem, send_sem, recv_sem,
):
    tile = tiles.shape[1]
    groups = rows_ref.shape[0]
    slots = tiles.shape[0] // groups
    gathered = (gathered0, gathered1)
    prefix = (prefix0, prefix1)
    sub = gathered0.shape[1]
    segment, classes = cot_ref.shape
    half = segment // 2
    per = segment // sub
    row, col = lax.axis_index("row"), lax.axis_index("col")
    y, x = row // RING, row % RING
    z, core = col // 2, col % 2
    a = x + core * (y - x)
    b = y + core * (x - y)
    step_a = 1 + 3 * core
    step_b = 4 - 3 * core

    def at(da, db):
        return ((a + da) % RING) * step_a + ((b + db) % RING) * step_b

    def device(da, db):
        return {"row": at(da, db), "col": col}

    a_right, a_left = device(1, 0), device(3, 0)
    b_right, b_left = device(0, 1), device(0, 3)
    z_right = {"row": row, "col": ((z + 1) % RING) * 2 + core}
    z_left = {"row": row, "col": ((z + 3) % RING) * 2 + core}
    twin = {"row": row, "col": z * 2 + (1 - core)}

    barrier = pltpu.get_barrier_semaphore()
    for other in (a_right, a_left, b_right, b_left, z_right, z_left, twin):
        pl.semaphore_signal(barrier, inc=1, device_id=other, device_id_type=MESH)

    small = [
        pltpu.make_async_copy(source, target, small_sem.at[q])
        for q, (source, target) in enumerate((
            (cot_hbm, cot_ref), (seed_hbm, seed_ref), (rows_hbm, rows_ref), (cols_hbm, cols_ref), (scale_hbm, scale_ref)
        ))
    ]
    for load in small:
        load.start()
    loads = [
        pltpu.make_async_copy(
            tiles_hbm.at[pl.ds(q * tiles.shape[0] // 4, tiles.shape[0] // 4)],
            tiles.at[pl.ds(q * tiles.shape[0] // 4, tiles.shape[0] // 4)],
            tile_sem.at[q],
        )
        for q in range(4)
    ]
    for load in loads:
        load.start()

    small[0].wait()
    small[1].wait()
    for block in range(segment // tile):
        seeds = jnp.broadcast_to(seed_ref[block : block + 1, :], (tile, tile)).T
        lanes = lax.broadcasted_iota(jnp.int32, (tile, tile), 1)
        rows = slice(block * tile, (block + 1) * tile)
        for c in range(classes // tile):
            lane = slice(c * tile, (c + 1) * tile)
            kept = jnp.where(seeds == lanes + c * tile, 0.0, 1.0)
            keep[rows, lane] = kept
            masked = (cot_ref[rows, lane].astype(F32) * kept).astype(BF16)
            for part in range(tile // sub):
                gathered0[col * per + block * (tile // sub) + part, :, lane] = masked[part * sub : (part + 1) * sub]

    pl.semaphore_wait(barrier, 7)

    def gather_copy(p, j):
        seg_left = ((z + 3) % RING) * 2 + core
        seg_right = ((z + 1) % RING) * 2 + core
        seg_far = ((z + 2) % RING) * 2 + core
        seg, top, size, target = (
            (col, 0, half, z_right),
            (col, half, half, z_right),
            (col, half, half, z_left),
            (col, 0, half, z_left),
            (seg_left, 0, half, z_right),
            (seg_right, half, half, z_left),
            (col, 0, segment, twin),
            (seg_left, 0, half, twin),
            (seg_left, half, half, twin),
            (seg_right, half, half, twin),
            (seg_right, 0, half, twin),
            (seg_far, 0, half, twin),
            (seg_far, half, half, twin),
        )[j]
        window = gathered[p].at[pl.ds(seg * per + top // sub, size // sub)]
        sem = N_REDUCE + j
        return pltpu.make_async_remote_copy(
            src_ref=window, dst_ref=window, send_sem=send_sem.at[p, sem], recv_sem=recv_sem.at[p, sem],
            device_id=target, device_id_type=MESH,
        )

    def arrival(p, j):
        seg_left = ((z + 3) % RING) * 2 + core
        seg_right = ((z + 1) % RING) * 2 + core
        seg_far = ((z + 2) % RING) * 2 + core
        flip = 1 - 2 * core
        seg, top, size = (
            (seg_left, 0, half),
            (seg_left, half, half),
            (seg_right, half, half),
            (seg_right, 0, half),
            (seg_far, 0, half),
            (seg_far, half, half),
            (col + flip, 0, segment),
            (seg_left + flip, 0, half),
            (seg_left + flip, half, half),
            (seg_right + flip, half, half),
            (seg_right + flip, 0, half),
            (seg_far + flip, 0, half),
            (seg_far + flip, half, half),
        )[j]
        window = gathered[p].at[pl.ds(seg * per + top // sub, size // sub)]
        sem = N_REDUCE + j
        return pltpu.make_async_remote_copy(
            src_ref=window, dst_ref=window, send_sem=send_sem.at[p, sem], recv_sem=recv_sem.at[p, sem],
            device_id=twin, device_id_type=MESH,
        )

    upper, lower = pl.ds(0, half), pl.ds(half, half)

    def reduce_copy(p, i, kind, right, left):
        piece = 3 * i + kind // 2
        rows = (upper, lower, upper, lower, lower, upper)[kind]
        sem = 6 * i + kind
        return pltpu.make_async_remote_copy(
            src_ref=sent.at[p, piece, rows], dst_ref=got.at[p, piece, rows],
            send_sem=send_sem.at[p, sem], recv_sem=recv_sem.at[p, sem],
            device_id=(right, left, right, right, left, left)[kind], device_id_type=MESH,
        )

    def along_a(p, i, kind):
        return reduce_copy(p, i, kind, a_right, a_left)

    def along_b(p, kind):
        return reduce_copy(p, 4, kind, b_right, b_left)

    def start_gather(p):
        for j in (0, 2, 6, 1, 3):
            gather_copy(p, j).start()

    def finish_gather(p):
        arrival(p, 0).wait_recv()
        gather_copy(p, 4).start()
        gather_copy(p, 7).start()
        arrival(p, 2).wait_recv()
        gather_copy(p, 5).start()
        gather_copy(p, 9).start()
        arrival(p, 1).wait_recv()
        gather_copy(p, 8).start()
        arrival(p, 3).wait_recv()
        gather_copy(p, 10).start()
        arrival(p, 4).wait_recv()
        gather_copy(p, 11).start()
        arrival(p, 5).wait_recv()
        gather_copy(p, 12).start()
        for j in range(6, N_GATHER):
            arrival(p, j).wait_recv()

    start_gather(0)

    for load in small[2:]:
        load.wait()

    def sort_group(g, carry):
        keys, first, second = [], 0, 0
        for k in range(slots):
            c = cols_ref[g, k]
            keys.append(c * 8192 + (k * 256 + rows_ref[g, k] * 8 + scale_ref[g, k]))
            first = first + ((2 - c) >> 1)
            second = second + (1 - (c >> 1))
        for i, j in sort_network(slots):
            keys[i], keys[j] = jnp.minimum(keys[i], keys[j]), jnp.maximum(keys[i], keys[j])
        for k in range(slots):
            order[g, k] = ((keys[k] >> 8) & 31) + g * slots
            order[g, slots + k] = (keys[k] >> 3) & 31
            order[g, 2 * slots + k] = keys[k] & 7
        order[g, 3 * slots] = first
        order[g, 3 * slots + 1] = second
        return carry

    lax.fori_loop(0, groups, sort_group, 0)

    def product(p, u, target):
        total = jnp.zeros((tile, classes), F32)
        prefix[u][0] = total
        for q in range(slots):
            source = order[target, slots + q] * (tile // sub)
            labels = jnp.concatenate([gathered[p][source + part] for part in range(tile // sub)], axis=0)
            term = lax.dot_general(tiles[order[target, q]], labels, TN, preferred_element_type=F32)
            total = total + term * order[target, 2 * slots + q].astype(F32)
            prefix[u][q + 1] = total
        one = prefix[u][order[target, 3 * slots]]
        two = prefix[u][order[target, 3 * slots + 1]]
        current[u, 0:tile] = one
        current[u, tile : 2 * tile] = two - one
        current[u, 2 * tile : 3 * tile] = total - two

    def summed(p, i, rows, from_left, from_right):
        along_a(p, i, from_left).wait_recv()
        along_a(p, i, from_right).wait_recv()
        return own[i, rows] + got[p, 3 * i + 1, rows].astype(F32) + got[p, 3 * i + 2, rows].astype(F32)

    for p in range(2):
        finish_gather(p)
        if p == 0:
            for load in loads:
                load.wait()

        def send_whole(u, i):
            sent[p, 3 * i] = current[u].astype(BF16)
            along_a(p, i, 0).start()
            along_a(p, i, 1).start()

        for i in range(2):
            product(p, i, at(2, 2 + i * (i + 1) // 2))
            send_whole(i, i)

        def one_step(s, carry):
            far = s < 2
            side = jnp.logical_and(s >= 2, s < 6)
            i0 = jnp.where(far, 2 * s, jnp.where(side, s - 2, 2 * s - 12))
            i1 = jnp.where(side, i0, i0 + 1)
            da0 = jnp.where(far, 2, jnp.where(side, 1, 0))
            da1 = jnp.where(far, 2, jnp.where(side, 3, 0))
            product(p, 0, at(da0, 2 + i0 * (i0 + 1) // 2))
            product(p, 1, at(da1, 2 + i1 * (i1 + 1) // 2))

            @pl.when(far)
            def _():
                for u in range(2):
                    send_whole(u, 2 * s + u)

            @pl.when(side)
            def _():
                i = s - 2
                sent[p, 3 * i + 1, half:segment] = current[0, half:segment].astype(BF16)
                along_a(p, i, 3).start()
                sent[p, 3 * i + 2, 0:half] = current[1, 0:half].astype(BF16)
                along_a(p, i, 5).start()
                along_a(p, i, 0).wait_recv()
                sent[p, 3 * i + 1, 0:half] = (current[0, 0:half] + got[p, 3 * i, 0:half].astype(F32)).astype(BF16)
                along_a(p, i, 2).start()
                along_a(p, i, 1).wait_recv()
                sent[p, 3 * i + 2, half:segment] = (
                    current[1, half:segment] + got[p, 3 * i, half:segment].astype(F32)
                ).astype(BF16)
                along_a(p, i, 4).start()

            @pl.when(s >= 6)
            def _():
                own[2 * s - 12] = current[0]
                own[2 * s - 11] = current[1]

            @pl.when(s == 6)
            def _():
                sent[p, 12, upper] = summed(p, 0, upper, 2, 5).astype(BF16)
                along_b(p, 0).start()
                sent[p, 12, lower] = summed(p, 0, lower, 3, 4).astype(BF16)
                along_b(p, 1).start()

            return carry

        lax.fori_loop(1, 8, one_step, 0)

        sent[p, 14, upper] = summed(p, 1, upper, 2, 5).astype(BF16)
        along_b(p, 5).start()
        sent[p, 13, lower] = summed(p, 2, lower, 3, 4).astype(BF16)
        along_b(p, 3).start()
        if p == 1:
            for q in range(2):
                for j in range(N_GATHER):
                    gather_copy(q, j).wait_send()
            for kind in range(6):
                for i in range(4):
                    along_a(0, i, kind).wait_send()
                along_b(0, kind).wait_send()
        total = summed(p, 1, lower, 3, 4)
        along_b(p, 1).wait_recv()
        sent[p, 14, lower] = (total + got[p, 12, lower].astype(F32)).astype(BF16)
        along_b(p, 4).start()
        total = summed(p, 2, upper, 2, 5)
        along_b(p, 0).wait_recv()
        sent[p, 13, upper] = (total + got[p, 12, upper].astype(F32)).astype(BF16)
        along_b(p, 2).start()
        own[3, upper] = summed(p, 3, upper, 2, 5)
        own[3, lower] = summed(p, 3, lower, 3, 4)
        if p == 1:
            for kind in range(6):
                for i in range(4):
                    along_a(1, i, kind).wait_send()
        for top, from_left, from_right in ((0, 2, 5), (half, 3, 4)):
            rows = pl.ds(top, half)
            along_b(p, from_left).wait_recv()
            along_b(p, from_right).wait_recv()
            total = ALPHA * (own[3, rows] + got[p, 13, rows].astype(F32) + got[p, 14, rows].astype(F32))
            if p == 0:
                first = total.astype(BF16)
                masked = (first.astype(F32) * keep[rows]).astype(BF16)
                for part in range(half // sub):
                    gathered1[col * per + top // sub + part] = masked[part * sub : (part + 1) * sub]
                for j in (0,) if top == 0 else (2, 6, 1, 3):
                    gather_copy(1, j).start()
                first_ref[rows] = first
            else:
                label_ref[rows] = (
                    total + (1.0 - ALPHA) * keep[rows] * (cot_ref[rows].astype(F32) + first_ref[rows].astype(F32))
                ).astype(BF16)

    for kind in range(6):
        along_b(1, kind).wait_send()


def hand_over(first_in, label_in, first_out, label_out):
    first_out[...] = first_in[...]
    label_out[...] = label_in[...]


def local(cotangent, seed_label, tile_values, tile_rows, tile_cols, tile_scale):
    segment, classes = cotangent.shape
    _, _, groups, slots, tile, _ = tile_values.shape
    vmem = pl.BlockSpec(memory_space=pltpu.VMEM)
    out = jax.ShapeDtypeStruct((segment, classes), BF16)
    results = pl.pallas_call(
        kernel,
        out_shape=(out, out),
        in_specs=[pl.BlockSpec(memory_space=pltpu.HBM)] * 6,
        out_specs=(vmem, vmem),
        scratch_shapes=[
            pltpu.VMEM((segment, classes), BF16),
            pltpu.VMEM((segment // tile, tile), jnp.int32),
            pltpu.SMEM((groups, slots), jnp.int32),
            pltpu.SMEM((groups, slots), jnp.int32),
            pltpu.SMEM((groups, slots), jnp.int32),
            pltpu.SemaphoreType.DMA((5,)),
            pltpu.VMEM((groups * slots, tile, tile), BF16),
            pltpu.VMEM((2 * RING * segment // 64, 64, classes), BF16),
            pltpu.VMEM((2 * RING * segment // 64, 64, classes), BF16),
            pltpu.VMEM((slots + 1, tile, classes), F32),
            pltpu.VMEM((slots + 1, tile, classes), F32),
            pltpu.VMEM((2, segment, classes), F32),
            pltpu.VMEM((4, segment, classes), F32),
            pltpu.VMEM((2, 15, segment, classes), BF16),
            pltpu.VMEM((2, 15, segment, classes), BF16),
            pltpu.VMEM((segment, classes), F32),
            pltpu.SMEM((groups, 3 * slots + 2), jnp.int32),
            pltpu.SemaphoreType.DMA((4,)),
            pltpu.SemaphoreType.DMA((2, N_REDUCE + N_GATHER)),
            pltpu.SemaphoreType.DMA((2, N_REDUCE + N_GATHER)),
        ],
        compiler_params=pltpu.CompilerParams(
            collective_id=0, has_side_effects=True, vmem_limit_bytes=42 * 1024 * 1024
        ),
        name="propagate_twice",
    )(
        pltpu.with_memory_space_constraint(cotangent, pltpu.HBM),
        pltpu.with_memory_space_constraint(seed_label.reshape(segment // tile, tile), pltpu.HBM),
        pltpu.with_memory_space_constraint(tile_rows[0, 0], pltpu.HBM),
        pltpu.with_memory_space_constraint(tile_cols[0, 0], pltpu.HBM),
        pltpu.with_memory_space_constraint(tile_scale[0, 0], pltpu.HBM),
        tile_values.reshape(groups * slots, tile, tile),
    )
    return pl.pallas_call(
        hand_over,
        out_shape=(out, out),
        in_specs=[vmem, vmem],
        out_specs=(vmem, vmem),
        compiler_params=pltpu.CompilerParams(vmem_limit_bytes=4 * 1024 * 1024),
        name="finish_results",
    )(*results)


def solution(mesh):
    return jax.shard_map(
        local,
        mesh=mesh,
        in_specs=(
            P(("row", "col"), None),
            P(("row", "col")),
            P("row", "col", None, None, None, None),
            P("row", "col", None, None),
            P("row", "col", None, None),
            P("row", "col", None, None),
        ),
        out_specs=(P(("row", "col"), None), P(("row", "col"), None)),
        check_vma=False,
    )
```

```python
import jax
import jax.numpy as jnp
from jax import lax
from jax.experimental import pallas as pl
from jax.experimental.pallas import tpu as pltpu
from jax.sharding import PartitionSpec as P

ALPHA = 0.9
MESH = pl.DeviceIdType.MESH
F32 = jnp.float32
BF16 = jnp.bfloat16
RING = 4
TN = (((0,), (0,)), ((), ()))
N_REDUCE = 30
N_GATHER = 13


def sort_network(count):
    size = 1
    while size < count:
        size *= 2
    pairs = []
    p = 1
    while p < size:
        k = p
        while k >= 1:
            for j in range(k % p, size - k, 2 * k):
                for i in range(min(k, size - j - k)):
                    if (i + j) // (p * 2) == (i + j + k) // (p * 2) and i + j + k < count:
                        pairs.append((i + j, i + j + k))
            k //= 2
        p *= 2
    return pairs


def kernel(
    cot_hbm, seed_hbm, rows_hbm, cols_hbm, scale_hbm, tiles_hbm,
    first_ref, label_ref,
    cot_ref, seed_ref, rows_ref, cols_ref, scale_ref, small_sem, tiles, gathered0, gathered1, prefix0, prefix1, current, own, sent, got, keep, order,
    tile_sem, send_sem, recv_sem,
):
    tile = tiles.shape[1]
    groups = rows_ref.shape[0]
    slots = tiles.shape[0] // groups
    gathered = (gathered0, gathered1)
    prefix = (prefix0, prefix1)
    sub = gathered0.shape[1]
    segment, classes = cot_ref.shape
    half = segment // 2
    per = segment // sub
    row, col = lax.axis_index("row"), lax.axis_index("col")
    y, x = row // RING, row % RING
    z, core = col // 2, col % 2
    a = x + core * (y - x)
    b = y + core * (x - y)
    step_a = 1 + 3 * core
    step_b = 4 - 3 * core

    def at(da, db):
        return ((a + da) % RING) * step_a + ((b + db) % RING) * step_b

    def device(da, db):
        return {"row": at(da, db), "col": col}

    a_right, a_left = device(1, 0), device(3, 0)
    b_right, b_left = device(0, 1), device(0, 3)
    z_right = {"row": row, "col": ((z + 1) % RING) * 2 + core}
    z_left = {"row": row, "col": ((z + 3) % RING) * 2 + core}
    twin = {"row": row, "col": z * 2 + (1 - core)}

    barrier = pltpu.get_barrier_semaphore()
    for other in (a_right, a_left, b_right, b_left, z_right, z_left, twin):
        pl.semaphore_signal(barrier, inc=1, device_id=other, device_id_type=MESH)

    small = [
        pltpu.make_async_copy(source, target, small_sem.at[q])
        for q, (source, target) in enumerate((
            (cot_hbm, cot_ref), (seed_hbm, seed_ref), (rows_hbm, rows_ref), (cols_hbm, cols_ref), (scale_hbm, scale_ref)
        ))
    ]
    for load in small:
        load.start()
    loads = [
        pltpu.make_async_copy(
            tiles_hbm.at[pl.ds(q * tiles.shape[0] // 4, tiles.shape[0] // 4)],
            tiles.at[pl.ds(q * tiles.shape[0] // 4, tiles.shape[0] // 4)],
            tile_sem.at[q],
        )
        for q in range(4)
    ]
    for load in loads:
        load.start()

    small[0].wait()
    small[1].wait()

    def gather_copy(p, j):
        seg_left = ((z + 3) % RING) * 2 + core
        seg_right = ((z + 1) % RING) * 2 + core
        seg_far = ((z + 2) % RING) * 2 + core
        seg, top, size, target = (
            (col, 0, half, z_right),
            (col, half, half, z_right),
            (col, half, half, z_left),
            (col, 0, half, z_left),
            (seg_left, 0, half, z_right),
            (seg_right, half, half, z_left),
            (col, 0, segment, twin),
            (seg_left, 0, half, twin),
            (seg_left, half, half, twin),
            (seg_right, half, half, twin),
            (seg_right, 0, half, twin),
            (seg_far, 0, half, twin),
            (seg_far, half, half, twin),
        )[j]
        window = gathered[p].at[pl.ds(seg * per + top // sub, size // sub)]
        sem = N_REDUCE + j
        return pltpu.make_async_remote_copy(
            src_ref=window, dst_ref=window, send_sem=send_sem.at[p, sem], recv_sem=recv_sem.at[p, sem],
            device_id=target, device_id_type=MESH,
        )

    def arrival(p, j):
        seg_left = ((z + 3) % RING) * 2 + core
        seg_right = ((z + 1) % RING) * 2 + core
        seg_far = ((z + 2) % RING) * 2 + core
        flip = 1 - 2 * core
        seg, top, size = (
            (seg_left, 0, half),
            (seg_left, half, half),
            (seg_right, half, half),
            (seg_right, 0, half),
            (seg_far, 0, half),
            (seg_far, half, half),
            (col + flip, 0, segment),
            (seg_left + flip, 0, half),
            (seg_left + flip, half, half),
            (seg_right + flip, half, half),
            (seg_right + flip, 0, half),
            (seg_far + flip, 0, half),
            (seg_far + flip, half, half),
        )[j]
        window = gathered[p].at[pl.ds(seg * per + top // sub, size // sub)]
        sem = N_REDUCE + j
        return pltpu.make_async_remote_copy(
            src_ref=window, dst_ref=window, send_sem=send_sem.at[p, sem], recv_sem=recv_sem.at[p, sem],
            device_id=twin, device_id_type=MESH,
        )

    upper, lower = pl.ds(0, half), pl.ds(half, half)

    def reduce_copy(p, i, kind, right, left):
        piece = 3 * i + kind // 2
        rows = (upper, lower, upper, lower, lower, upper)[kind]
        sem = 6 * i + kind
        return pltpu.make_async_remote_copy(
            src_ref=sent.at[p, piece, rows], dst_ref=got.at[p, piece, rows],
            send_sem=send_sem.at[p, sem], recv_sem=recv_sem.at[p, sem],
            device_id=(right, left, right, right, left, left)[kind], device_id_type=MESH,
        )

    def along_a(p, i, kind):
        return reduce_copy(p, i, kind, a_right, a_left)

    def along_b(p, kind):
        return reduce_copy(p, 4, kind, b_right, b_left)

    def finish_gather(p):
        arrival(p, 0).wait_recv()
        gather_copy(p, 4).start()
        gather_copy(p, 7).start()
        arrival(p, 2).wait_recv()
        gather_copy(p, 5).start()
        gather_copy(p, 9).start()
        arrival(p, 1).wait_recv()
        gather_copy(p, 8).start()
        arrival(p, 3).wait_recv()
        gather_copy(p, 10).start()
        arrival(p, 4).wait_recv()
        gather_copy(p, 11).start()
        arrival(p, 5).wait_recv()
        gather_copy(p, 12).start()
        for j in range(6, N_GATHER):
            arrival(p, j).wait_recv()

    for block in range(segment // tile):
        seeds = jnp.broadcast_to(seed_ref[block : block + 1, :], (tile, tile)).T
        lanes = lax.broadcasted_iota(jnp.int32, (tile, tile), 1)
        rows = slice(block * tile, (block + 1) * tile)
        for c in range(classes // tile):
            lane = slice(c * tile, (c + 1) * tile)
            kept = jnp.where(seeds == lanes + c * tile, 0.0, 1.0)
            keep[rows, lane] = kept
            masked = (cot_ref[rows, lane].astype(F32) * kept).astype(BF16)
            for part in range(tile // sub):
                gathered0[col * per + block * (tile // sub) + part, :, lane] = masked[part * sub : (part + 1) * sub]
        if block == 1:
            pl.semaphore_wait(barrier, 7)
            gather_copy(0, 0).start()
    for j in (2, 6, 1, 3):
        gather_copy(0, j).start()

    for load in small[2:]:
        load.wait()

    def sort_group(g, carry):
        keys, first, second = [], 0, 0
        for k in range(slots):
            c = cols_ref[g, k]
            keys.append(c * 8192 + (k * 256 + rows_ref[g, k] * 8 + scale_ref[g, k]))
            first = first + ((2 - c) >> 1)
            second = second + (1 - (c >> 1))
        for i, j in sort_network(slots):
            keys[i], keys[j] = jnp.minimum(keys[i], keys[j]), jnp.maximum(keys[i], keys[j])
        for k in range(slots):
            order[g, k] = ((keys[k] >> 8) & 31) + g * slots
            order[g, slots + k] = (keys[k] >> 3) & 31
            order[g, 2 * slots + k] = keys[k] & 7
        order[g, 3 * slots] = first
        order[g, 3 * slots + 1] = second
        return carry

    lax.fori_loop(0, groups, sort_group, 0)

    def product(p, u, target):
        total = jnp.zeros((tile, classes), F32)
        prefix[u][0] = total
        for q in range(slots):
            source = order[target, slots + q] * (tile // sub)
            labels = jnp.concatenate([gathered[p][source + part] for part in range(tile // sub)], axis=0)
            term = lax.dot_general(tiles[order[target, q]], labels, TN, preferred_element_type=F32)
            total = total + term * order[target, 2 * slots + q].astype(F32)
            prefix[u][q + 1] = total
        one = prefix[u][order[target, 3 * slots]]
        two = prefix[u][order[target, 3 * slots + 1]]
        current[u, 0:tile] = one
        current[u, tile : 2 * tile] = two - one
        current[u, 2 * tile : 3 * tile] = total - two

    def summed(p, i, rows, from_left, from_right):
        along_a(p, i, from_left).wait_recv()
        along_a(p, i, from_right).wait_recv()
        return own[i, rows] + got[p, 3 * i + 1, rows].astype(F32) + got[p, 3 * i + 2, rows].astype(F32)

    for p in range(2):
        finish_gather(p)
        if p == 0:
            for load in loads:
                load.wait()

        def send_whole(u, i):
            sent[p, 3 * i] = current[u].astype(BF16)
            along_a(p, i, 0).start()
            along_a(p, i, 1).start()

        for i in range(2):
            product(p, i, at(2, 2 + i * (i + 1) // 2))
            send_whole(i, i)

        def one_step(s, carry):
            far = s < 2
            side = jnp.logical_and(s >= 2, s < 6)
            i0 = jnp.where(far, 2 * s, jnp.where(side, s - 2, 2 * s - 12))
            i1 = jnp.where(side, i0, i0 + 1)
            da0 = jnp.where(far, 2, jnp.where(side, 1, 0))
            da1 = jnp.where(far, 2, jnp.where(side, 3, 0))
            product(p, 0, at(da0, 2 + i0 * (i0 + 1) // 2))
            product(p, 1, at(da1, 2 + i1 * (i1 + 1) // 2))

            @pl.when(far)
            def _():
                for u in range(2):
                    send_whole(u, 2 * s + u)

            @pl.when(side)
            def _():
                i = s - 2
                sent[p, 3 * i + 1, half:segment] = current[0, half:segment].astype(BF16)
                along_a(p, i, 3).start()
                sent[p, 3 * i + 2, 0:half] = current[1, 0:half].astype(BF16)
                along_a(p, i, 5).start()
                along_a(p, i, 0).wait_recv()
                sent[p, 3 * i + 1, 0:half] = (current[0, 0:half] + got[p, 3 * i, 0:half].astype(F32)).astype(BF16)
                along_a(p, i, 2).start()
                along_a(p, i, 1).wait_recv()
                sent[p, 3 * i + 2, half:segment] = (
                    current[1, half:segment] + got[p, 3 * i, half:segment].astype(F32)
                ).astype(BF16)
                along_a(p, i, 4).start()

            @pl.when(s >= 6)
            def _():
                own[2 * s - 12] = current[0]
                own[2 * s - 11] = current[1]

            @pl.when(s == 6)
            def _():
                sent[p, 12, upper] = summed(p, 0, upper, 2, 5).astype(BF16)
                along_b(p, 0).start()
                sent[p, 12, lower] = summed(p, 0, lower, 3, 4).astype(BF16)
                along_b(p, 1).start()

            return carry

        lax.fori_loop(1, 8, one_step, 0)

        sent[p, 14, upper] = summed(p, 1, upper, 2, 5).astype(BF16)
        along_b(p, 5).start()
        sent[p, 13, lower] = summed(p, 2, lower, 3, 4).astype(BF16)
        along_b(p, 3).start()
        if p == 1:
            for q in range(2):
                for j in range(N_GATHER):
                    gather_copy(q, j).wait_send()
            for kind in range(6):
                for i in range(4):
                    along_a(0, i, kind).wait_send()
                along_b(0, kind).wait_send()
        total = summed(p, 1, lower, 3, 4)
        along_b(p, 1).wait_recv()
        sent[p, 14, lower] = (total + got[p, 12, lower].astype(F32)).astype(BF16)
        along_b(p, 4).start()
        total = summed(p, 2, upper, 2, 5)
        along_b(p, 0).wait_recv()
        sent[p, 13, upper] = (total + got[p, 12, upper].astype(F32)).astype(BF16)
        along_b(p, 2).start()
        own[3, upper] = summed(p, 3, upper, 2, 5)
        own[3, lower] = summed(p, 3, lower, 3, 4)
        if p == 1:
            for kind in range(6):
                for i in range(4):
                    along_a(1, i, kind).wait_send()
        for top, from_left, from_right in ((0, 2, 5), (half, 3, 4)):
            rows = pl.ds(top, half)
            along_b(p, from_left).wait_recv()
            along_b(p, from_right).wait_recv()
            total = ALPHA * (own[3, rows] + got[p, 13, rows].astype(F32) + got[p, 14, rows].astype(F32))
            if p == 0:
                first = total.astype(BF16)
                masked = (first.astype(F32) * keep[rows]).astype(BF16)
                for part in range(half // sub):
                    gathered1[col * per + top // sub + part] = masked[part * sub : (part + 1) * sub]
                for j in (0,) if top == 0 else (2, 6, 1, 3):
                    gather_copy(1, j).start()
                first_ref[rows] = first
            else:
                label_ref[rows] = (
                    total + (1.0 - ALPHA) * keep[rows] * (cot_ref[rows].astype(F32) + first_ref[rows].astype(F32))
                ).astype(BF16)

    for kind in range(6):
        along_b(1, kind).wait_send()


def hand_over(first_in, label_in, first_out, label_out):
    first_out[...] = first_in[...]
    label_out[...] = label_in[...]


def local(cotangent, seed_label, tile_values, tile_rows, tile_cols, tile_scale):
    segment, classes = cotangent.shape
    _, _, groups, slots, tile, _ = tile_values.shape
    vmem = pl.BlockSpec(memory_space=pltpu.VMEM)
    out = jax.ShapeDtypeStruct((segment, classes), BF16)
    results = pl.pallas_call(
        kernel,
        out_shape=(out, out),
        in_specs=[pl.BlockSpec(memory_space=pltpu.HBM)] * 6,
        out_specs=(vmem, vmem),
        scratch_shapes=[
            pltpu.VMEM((segment, classes), BF16),
            pltpu.VMEM((segment // tile, tile), jnp.int32),
            pltpu.SMEM((groups, slots), jnp.int32),
            pltpu.SMEM((groups, slots), jnp.int32),
            pltpu.SMEM((groups, slots), jnp.int32),
            pltpu.SemaphoreType.DMA((5,)),
            pltpu.VMEM((groups * slots, tile, tile), BF16),
            pltpu.VMEM((2 * RING * segment // 64, 64, classes), BF16),
            pltpu.VMEM((2 * RING * segment // 64, 64, classes), BF16),
            pltpu.VMEM((slots + 1, tile, classes), F32),
            pltpu.VMEM((slots + 1, tile, classes), F32),
            pltpu.VMEM((2, segment, classes), F32),
            pltpu.VMEM((4, segment, classes), F32),
            pltpu.VMEM((2, 15, segment, classes), BF16),
            pltpu.VMEM((2, 15, segment, classes), BF16),
            pltpu.VMEM((segment, classes), F32),
            pltpu.SMEM((groups, 3 * slots + 2), jnp.int32),
            pltpu.SemaphoreType.DMA((4,)),
            pltpu.SemaphoreType.DMA((2, N_REDUCE + N_GATHER)),
            pltpu.SemaphoreType.DMA((2, N_REDUCE + N_GATHER)),
        ],
        compiler_params=pltpu.CompilerParams(
            collective_id=0, has_side_effects=True, vmem_limit_bytes=42 * 1024 * 1024
        ),
        name="propagate_twice",
    )(
        pltpu.with_memory_space_constraint(cotangent, pltpu.HBM),
        pltpu.with_memory_space_constraint(seed_label.reshape(segment // tile, tile), pltpu.HBM),
        pltpu.with_memory_space_constraint(tile_rows[0, 0], pltpu.HBM),
        pltpu.with_memory_space_constraint(tile_cols[0, 0], pltpu.HBM),
        pltpu.with_memory_space_constraint(tile_scale[0, 0], pltpu.HBM),
        tile_values.reshape(groups * slots, tile, tile),
    )
    return pl.pallas_call(
        hand_over,
        out_shape=(out, out),
        in_specs=[vmem, vmem],
        out_specs=(vmem, vmem),
        compiler_params=pltpu.CompilerParams(vmem_limit_bytes=4 * 1024 * 1024),
        name="finish_results",
    )(*results)


def solution(mesh):
    return jax.shard_map(
        local,
        mesh=mesh,
        in_specs=(
            P(("row", "col"), None),
            P(("row", "col")),
            P("row", "col", None, None, None, None),
            P("row", "col", None, None),
            P("row", "col", None, None),
            P("row", "col", None, None),
        ),
        out_specs=(P(("row", "col"), None), P(("row", "col"), None)),
        check_vma=False,
    )
```
